128 devices in a mesh: row: 4 (over x), col: 32 (over z, y, core).
Axes of the slice: x: 4, y: 4, z: 4, core: 2. Of those that a mesh axis runs over, the one named last changes fastest.
Arguments:
- cells: float32 [128, 128, 128], P(('row', 'col')), may hold values from 0 to 1
- target: float32 [1024, 12288], P('row', 'col'), may hold values from 0 to 1
- row_taps: bfloat16 [24, 2, 35], replicated, may hold values from -1 to 1
- col_taps: bfloat16 [24, 2, 35], replicated, may hold values from -1 to 1
- socs: float32 [12], replicated, may hold values from 0.05 to 1
- cell_of_block: int32 [8, 96], P('row', 'col'), may hold values from 0 to 127
- owner_map: int32 [128], replicated, may hold values from 0 to 127, each once
Outputs:
- cell_gradient: float32 [128, 128, 128], P(('row', 'col'))
- new_mask: float32 [1024, 12288], P('row', 'col')
The draws below stay inside these ranges and needn't reach their ends.
Inputs may be any that keep to these rules, and one draw needn't show every extreme that they name: `owner_map`: every store position appears exactly once.
All inputs are finite; a program needn't handle non-finite values.
Results may differ from the reference program's by a relative error of at most 0.0063.
Values may be sent and summed in bfloat16 or wider, within the bound.
No kernel may reach another device: no remote copies, remote signals or barrier semaphores. Data moves between devices by JAX's collectives and lax.ppermute only.
A program may use at most 64 MiB of HBM per device.

```python
import math
import jax
import jax.numpy as jnp
import numpy as np
from jax import lax

KERN = 12
CHAN = 24
TAPS = 35
BLK = 128
CELLS = 128
HEIGHT = 1024
WIDTH = 12288
NBR = 8
NBC = 96


def place_ends(values, stream_key, least, largest):
    index_at = [jax.random.randint(jax.random.fold_in(stream_key, axis), (), 0, length) for axis, length in enumerate(values.shape)]
    widest = values.shape.index(max(values.shape))
    neighbour = index_at[:widest] + [(index_at[widest] + 1) % values.shape[widest]] + index_at[widest + 1:]
    return values.at[tuple(index_at)].set(least).at[tuple(neighbour)].set(largest)


def block_levels(rng, dims, shards, least, top_value):
    level, own = 1.0, jax.random.fold_in(rng, 6)
    for axis_at, shards_of in shards:
        draws = jnp.exp(jax.random.uniform(jax.random.fold_in(own, axis_at), (shards_of,), jnp.float32, least / len(shards), top_value / len(shards)))
        level = level * jnp.repeat(draws, dims[axis_at] // shards_of).reshape([-1 if axis == axis_at else 1 for axis in range(len(dims))])
    return level


def rank_table(count, slope):
    portions = [(1 << 20) // math.isqrt(standing ** slope) + 1 for standing in range(1, count + 1)]
    deviation = 1 + sum(portions) // (1 << 30)
    return np.cumsum(np.array([max(1, weight // deviation) for weight in portions]))


def ranked(own_key, shape, count, skew):
    listing = rank_table(count, skew)
    pick = jax.random.randint(jax.random.fold_in(own_key, 1), shape, 0, int(listing[count - 1]))
    grade = jnp.searchsorted(jnp.asarray(listing, jnp.int32), pick, side="right")
    return jax.random.permutation(jax.random.fold_in(own_key, 2), count)[grade].astype(jnp.int32)


def gaussian(key, dims, scale, limit, kind=jnp.bfloat16):
    values = jax.random.normal(key, dims, jnp.float32) * scale
    return jnp.minimum(jnp.maximum(values, -limit), limit).astype(kind)


def setup_inputs(seed: int = 0) -> dict:
    key_list = jax.random.split(jax.random.key(seed), 8)
    cells = jnp.clip(1.0 * jax.random.uniform(key_list[0], (CELLS, BLK, BLK), jnp.float32) ** block_levels(key_list[0], (CELLS, BLK, BLK), ((0, 128),), -0.2, 0.2), 0.0, 1.0)
    target = jnp.clip(1.0 * jax.random.uniform(key_list[1], (HEIGHT, WIDTH), jnp.float32) ** block_levels(key_list[1], (HEIGHT, WIDTH), ((0, 4), (1, 32)), -0.2, 0.2), 0.0, 1.0)
    row_taps = gaussian(key_list[2], (CHAN, 2, TAPS), TAPS ** -0.5, 1.0)
    col_taps = gaussian(key_list[3], (CHAN, 2, TAPS), TAPS ** -0.5, 1.0)
    socs = jnp.clip(jnp.exp(jax.random.uniform(key_list[4], (KERN,), jnp.float32, math.log(0.05), math.log(1.0))), 0.05, 1.0)
    cell_of_block = place_ends(ranked(key_list[5], (NBR, NBC), CELLS, 1), jax.random.fold_in(key_list[5], 3), 0, CELLS - 1).astype(jnp.int32)
    owner_map = jax.random.permutation(key_list[6], CELLS).astype(jnp.int32)
    return {"cells": cells, "target": target, "row_taps": row_taps, "col_taps": col_taps, "socs": socs, "cell_of_block": cell_of_block, "owner_map": owner_map}


def separable(padded, row_part, col_part):
    kernel_cols = col_part.astype(jnp.float32)[:, None, None, :]
    columns = lax.conv_general_dilated(padded, kernel_cols, (1, 1), "VALID", precision=lax.Precision.HIGHEST)
    columns = lax.optimization_barrier(columns.astype(jnp.bfloat16)).astype(jnp.float32)
    kernel_rows = row_part.astype(jnp.float32)[None, :, :, None]
    result = lax.conv_general_dilated(columns, kernel_rows, (1, 1), "VALID", precision=lax.Precision.HIGHEST)
    return result[0, 0]


def assemble(blocks):
    return blocks.transpose(0, 2, 1, 3).reshape(NBR * BLK, NBC * BLK)


def reference(cells, target, row_taps, col_taps, socs, cell_of_block, owner_map):
    half = TAPS // 2
    positions = owner_map[cell_of_block]
    placed_blocks = cells[positions]
    placed = assemble(placed_blocks)
    mask = lax.optimization_barrier(placed.astype(jnp.bfloat16)).astype(jnp.float32)
    padded = jnp.pad(mask, half)[None, None]
    weights = socs / jnp.sum(socs)

    def light(total, k):
        field = separable(padded, row_taps[k], col_taps[k])
        return total + weights[k // 2] * field * field, None

    intensity, _ = lax.scan(light, jnp.zeros((HEIGHT, WIDTH), jnp.float32), jnp.arange(CHAN))
    resist = jax.nn.sigmoid(3.0 * (intensity - 1.3))
    error = 2.0 * (resist - target) * 3.0 * resist * (1.0 - resist)

    def adjoint(total, k):
        field = separable(padded, row_taps[k], col_taps[k])
        weighted = 2.0 * weights[k // 2] * field * error
        weighted = lax.optimization_barrier(weighted.astype(jnp.bfloat16)).astype(jnp.float32)
        wide = jnp.pad(weighted, half)[None, None]
        return total + separable(wide, row_taps[k][:, ::-1], col_taps[k][:, ::-1]), None

    slab_gradient, _ = lax.scan(adjoint, jnp.zeros((HEIGHT, WIDTH), jnp.float32), jnp.arange(CHAN))
    blocks = slab_gradient.reshape(NBR, BLK, NBC, BLK).transpose(0, 2, 1, 3).reshape(NBR * NBC, BLK, BLK)
    cell_gradient = jax.ops.segment_sum(blocks, positions.reshape(-1), num_segments=CELLS)
    new_blocks = placed_blocks - 0.05 * cell_gradient[positions]
    return cell_gradient, assemble(new_blocks)
```

```python
import jax
import jax.numpy as jnp
from jax import lax
from jax.experimental import pallas as pl
from jax.experimental.pallas import tpu as pltpu
from jax.sharding import PartitionSpec as P

AXES = ("row", "col")
ROWS, COLS = 4, 32
DEV = ROWS * COLS
BLK = 128
HALF = 17
WIN = BLK + 2 * HALF
TILE_R, TILE_C = 256, 384
EXT_R = 296
CHAN = 24
SLOTS = 16
BF, F32 = jnp.bfloat16, jnp.float32


def dot(a, b):
    return lax.dot_general(a, b, (((1,), (0,)), ((), ())), preferred_element_type=F32)


def iota(dim, shape=(DEV, BLK)):
    return lax.broadcasted_iota(jnp.int32, shape, dim)


def slot_ids(ids, holder):
    lane, dev = iota(1), iota(0)
    dev_row, dev_col = dev // COLS, dev % COLS
    upper = ids
    lower = pltpu.roll(ids, BLK - 3, 1)
    above = jnp.where(dev_row == 0, -1.0, pltpu.roll(lower, COLS, 0))
    below = jnp.where(dev_row == ROWS - 1, -1.0, pltpu.roll(upper, DEV - COLS, 0))
    third = jnp.where(holder >= BLK // 2, above, below)
    out = jnp.full((DEV, BLK), -1.0, F32)
    for p, part in enumerate((upper, lower, third)):
        left = jnp.where(dev_col == 0, -1.0, pltpu.roll(part, 1, 0))
        right = jnp.where(dev_col == COLS - 1, -1.0, pltpu.roll(part, DEV - 1, 0))
        here = pltpu.roll(part, 4 * p, 1) if p else part
        out = jnp.where((lane >= 4 * p) & (lane < 4 * p + 3), here, out)
        out = jnp.where(lane == 4 * p + 3, pltpu.roll(left, 4 * p + 1, 1), out)
        out = jnp.where(lane == 12 + p, pltpu.roll(right, 12 + p, 1), out)
    return out


def owner_select(owner_ref, transpose):
    if transpose:
        return (owner_ref[0:1, :] == iota(0)).astype(BF)
    return (owner_ref[...].T == iota(1)).astype(BF)


def columns_of(slots, s):
    return jnp.broadcast_to(slots[:, s : s + 1], (DEV, BLK))


def pick_kernel(holder_ref, table_ref, ids_ref, owner_ref, out_ref, held_ref, stage):
    lane = iota(1)
    slots = slot_ids(ids_ref[...].astype(F32), holder_ref[0])
    cell = lane.astype(F32)
    held = dot(owner_select(owner_ref, False), table_ref[...]).astype(BF)
    held_ref[...] = held

    def pick(s):
        return dot((columns_of(slots, s) == cell).astype(BF), held)

    for p in range(3):
        for q in range(3):
            stage[pl.ds(4 * p + q, DEV, stride=SLOTS), :] = pick(4 * p + q)
        halo = jnp.where(lane >= BLK // 2, pick(4 * p + 3), pick(12 + p))
        stage[pl.ds(4 * p + 3, DEV, stride=SLOTS), :] = halo
    for s in range(12, SLOTS):
        stage[pl.ds(s, DEV, stride=SLOTS), :] = jnp.zeros((DEV, BLK), F32)
    out_ref[...] = stage[...].astype(BF)


def toeplitz(taps_ref, m, shift_stride=1):
    base = jnp.broadcast_to(taps_ref[pl.ds(m, 1), :], (BLK, 2 * BLK))
    return pltpu.roll(base, 0, 1, stride=1, stride_axis=0).astype(BF)


def litho_kernel(
    weights_ref, recv_ref, target_ref, row_ref, row_rev_ref, col_ref, col_rev_ref,
    out_ref, stage, wide, mask, columns, field, light, grad, back_taps,
):
    stage[...] = recv_ref[...].astype(F32)
    for q in range(4):
        for p in range(3):
            wide[p * BLK : (p + 1) * BLK, q * BLK : (q + 1) * BLK] = stage[
                pl.ds(4 * p + q, DEV, stride=SLOTS), :
            ]
    mask[...] = pltpu.roll(pltpu.roll(wide[...], HALF, 1), HALF, 0)[:EXT_R].astype(BF)
    columns[:, EXT_R:, :] = jnp.zeros((2, 384 - EXT_R, TILE_C), BF)
    light[...] = jnp.zeros_like(light)

    def forward(k, carry):
        rolled = [toeplitz(col_rev_ref, 2 * k + r) for r in range(2)]
        col_matrix = jnp.concatenate(
            [
                jnp.concatenate([t[:, :BLK] for t in rolled], 1),
                jnp.concatenate([t[:, BLK:] for t in rolled], 1),
            ],
            0,
        )
        for q in range(3):
            made = dot(mask[:, q * BLK : (q + 2) * BLK], col_matrix).astype(BF)
            for r in range(2):
                columns[r, :EXT_R, q * BLK : (q + 1) * BLK] = made[:, r * BLK : (r + 1) * BLK]
        row_matrix = jnp.concatenate([toeplitz(row_ref, 2 * k + r) for r in range(2)], 1)
        weight = weights_ref[k // 2]
        for p in range(2):
            window = jnp.concatenate(
                [columns[r, p * BLK : (p + 2) * BLK, :] for r in range(2)], 0
            )
            made = dot(row_matrix, window)
            here = slice(p * BLK, (p + 1) * BLK)
            light[here] += weight * made * made
            field[k, here] = made
        return carry

    lax.fori_loop(0, CHAN, forward, 0)
    resist = jax.nn.sigmoid(3.0 * (light[...] - 1.3))
    light[...] = 2.0 * (resist - target_ref[...]) * 3.0 * resist * (1.0 - resist)
    grad[...] = jnp.zeros_like(grad)
    back_taps[...] = jnp.zeros_like(back_taps)

    def backward(k, carry):
        weighted = (2.0 * weights_ref[k // 2] * field[k] * light[...]).astype(BF)
        for r in range(2):
            rolled = toeplitz(row_rev_ref, 2 * k + r)
            top, bottom = rolled[:, :BLK], rolled[:, BLK:]
            at = r * EXT_R
            back_taps[at : at + BLK, :BLK] = top
            back_taps[at + BLK : at + 2 * BLK, BLK:] = top
            back_taps[at + BLK : at + 2 * BLK, :BLK] = bottom
            back_taps[at + 2 * BLK : at + EXT_R, BLK:] = bottom[: EXT_R - 2 * BLK]
        back = dot(back_taps[...], weighted).astype(BF)
        col_matrix = jnp.concatenate([toeplitz(col_ref, 2 * k + r) for r in range(2)], 0)
        for q in range(3):
            here = slice(q * BLK, (q + 1) * BLK)
            both = jnp.concatenate([back[:EXT_R, here], back[EXT_R:, here]], 1)
            grad[:EXT_R, q * BLK : (q + 2) * BLK] += dot(both, col_matrix)
        return carry

    lax.fori_loop(0, CHAN, backward, 0)
    wide[...] = pltpu.roll(pltpu.roll(grad[...], 384 - HALF, 0), 512 - HALF, 1)
    for q in range(4):
        for p in range(3):
            stage[pl.ds(4 * p + q, DEV, stride=SLOTS), :] = wide[
                p * BLK : (p + 1) * BLK, q * BLK : (q + 1) * BLK
            ]
    for s in range(12, SLOTS):
        stage[pl.ds(s, DEV, stride=SLOTS), :] = jnp.zeros((DEV, BLK), F32)
    out_ref[...] = stage[...].astype(BF)


def update_kernel(holder_ref, recv_ref, ids_ref, owner_ref, held_ref, out_ref, stage, out_stage):
    lane = iota(1)
    slots = slot_ids(ids_ref[...].astype(F32), holder_ref[0])
    slots_t = slots.T
    cell_down = iota(0).astype(F32)
    stage[...] = recv_ref[...].astype(F32)

    def gather(s, piece):
        select = (jnp.broadcast_to(slots_t[s : s + 1, :], (BLK, DEV)) == cell_down).astype(BF)
        return dot(select, stage[pl.ds(piece, DEV, stride=SLOTS), :].astype(BF))

    total = jnp.zeros((BLK, BLK), F32)
    from_left, from_right = total, total
    for p in range(3):
        for q in range(3):
            total += gather(4 * p + q, 4 * p + q)
        from_left += gather(4 * p + 3, 4 * p + 3)
        from_right += gather(12 + p, 4 * p + 3)
    total += jnp.where(lane >= BLK // 2, from_left, from_right)
    updated = (held_ref[...].astype(F32) - 0.05 * total).astype(BF)
    cell = lane.astype(F32)
    for p in range(2):
        for q in range(3):
            select = (columns_of(slots, 4 * p + q) == cell).astype(BF)
            out_stage[pl.ds(3 * p + q, DEV, stride=8), :] = dot(select, updated)
    by_owner = owner_select(owner_ref, True)
    out_stage[pl.ds(6, DEV, stride=8), :] = dot(by_owner, total.astype(BF))
    out_stage[pl.ds(7, DEV, stride=8), :] = jnp.zeros((DEV, BLK), F32)
    out_ref[...] = out_stage[...].astype(BF)


def unpack_kernel(recv_ref, grad_ref, mask_ref, stage):
    stage[...] = recv_ref[...].astype(F32)
    for p in range(2):
        for q in range(3):
            mask_ref[p * BLK : (p + 1) * BLK, q * BLK : (q + 1) * BLK] = stage[
                pl.ds(3 * p + q, DEV, stride=8), :
            ]
    grad_ref[...] = stage[pl.ds(6, DEV, stride=8), :]


SMEM = pl.BlockSpec(memory_space=pltpu.SMEM)
VMEM = pl.BlockSpec(memory_space=pltpu.VMEM)


def call(kernel, out_shape, in_specs, scratch, name):
    return pl.pallas_call(
        kernel,
        out_shape=out_shape,
        in_specs=in_specs,
        out_specs=jax.tree.map(lambda _: VMEM, out_shape),
        scratch_shapes=scratch,
        name=name,
    )


def exchange(x):
    return lax.all_to_all(x, AXES, 0, 0, tiled=True)


def per_device(cells, target, row_taps, col_taps, socs, cell_of_block, owner_map):
    struct = jax.ShapeDtypeStruct
    holder = (lax.axis_index("row") * COLS + lax.axis_index("col")).astype(jnp.int32).reshape(1)
    weights = socs / jnp.sum(socs)
    owner = jnp.broadcast_to(owner_map[None, :], (DEV, DEV))

    def spread(taps, reverse):
        flat = taps.reshape(2 * CHAN, 2 * HALF + 1).astype(F32)
        gap = jnp.zeros((2 * CHAN, 2 * BLK - 2 * HALF - 1), F32)
        if reverse:
            return jnp.concatenate([flat[:, :1], gap, flat[:, :0:-1]], 1)
        return jnp.concatenate([flat, gap], 1)

    own_ids = jnp.pad(cell_of_block.reshape(1, 6).astype(BF), ((0, 0), (0, BLK - 6)))
    first = jnp.stack([cells[0].astype(BF), jnp.broadcast_to(own_ids, (BLK, BLK))], 1)
    first = exchange(first)
    table, ids = first[:, 0], first[:, 1]

    picked, held = call(
        pick_kernel,
        (struct((DEV * SLOTS, BLK), BF), struct((BLK, BLK), BF)),
        [SMEM, VMEM, VMEM, VMEM],
        [pltpu.VMEM((DEV * SLOTS, BLK), F32)],
        "pick",
    )(holder, table, ids, owner)
    received = exchange(picked.reshape(DEV, SLOTS, BLK)).reshape(DEV * SLOTS, BLK)

    pieces = call(
        litho_kernel,
        struct((DEV * SLOTS, BLK), BF),
        [SMEM] + [VMEM] * 6,
        [
            pltpu.VMEM((DEV * SLOTS, BLK), F32),
            pltpu.VMEM((384, 512), F32),
            pltpu.VMEM((EXT_R, 512), BF),
            pltpu.VMEM((2, 384, TILE_C), BF),
            pltpu.VMEM((CHAN, TILE_R, TILE_C), F32),
            pltpu.VMEM((TILE_R, TILE_C), F32),
            pltpu.VMEM((384, 512), F32),
            pltpu.VMEM((2 * EXT_R, TILE_R), BF),
        ],
        "litho",
    )(
        weights, received, target,
        spread(row_taps, False), spread(row_taps, True),
        spread(col_taps, False), spread(col_taps, True),
    )
    pieces = exchange(pieces.reshape(DEV, SLOTS, BLK)).reshape(DEV * SLOTS, BLK)

    results = call(
        update_kernel,
        struct((DEV * 8, BLK), BF),
        [SMEM] + [VMEM] * 4,
        [pltpu.VMEM((DEV * SLOTS, BLK), F32), pltpu.VMEM((DEV * 8, BLK), F32)],
        "update",
    )(holder, pieces, ids, owner, held)
    results = exchange(results.reshape(DEV, 8, BLK)).reshape(DEV * 8, BLK)

    gradient, new_mask = call(
        unpack_kernel,
        (struct((BLK, BLK), F32), struct((TILE_R, TILE_C), F32)),
        [VMEM],
        [pltpu.VMEM((DEV * 8, BLK), F32)],
        "unpack",
    )(results)
    return gradient.reshape(1, BLK, BLK), new_mask


def solution(mesh):
    in_specs = (P(AXES, None, None), P("row", "col"), P(), P(), P(), P("row", "col"), P())
    out_specs = (P(AXES, None, None), P("row", "col"))
    return jax.shard_map(
        per_device, mesh=mesh, in_specs=in_specs, out_specs=out_specs, check_vma=False
    )
```

```python
import jax
import jax.numpy as jnp
from jax import lax
from jax.experimental import pallas as pl
from jax.experimental.pallas import tpu as pltpu
from jax.sharding import PartitionSpec as P

AXES = ("row", "col")
ROWS, COLS = 4, 32
DEV = ROWS * COLS
BLK = 128
HALF = 17
WIN = BLK + 2 * HALF
TILE_R, TILE_C = 256, 384
EXT_R = 296
CHAN = 24
SLOTS = 16
BF, F32 = jnp.bfloat16, jnp.float32


def dot(a, b):
    return lax.dot_general(a, b, (((1,), (0,)), ((), ())), preferred_element_type=F32)


def iota(dim, shape=(DEV, BLK)):
    return lax.broadcasted_iota(jnp.int32, shape, dim)


def slot_ids(ids, holder):
    lane, dev = iota(1), iota(0)
    dev_row, dev_col = dev // COLS, dev % COLS
    upper = ids
    lower = pltpu.roll(ids, BLK - 3, 1)
    above = jnp.where(dev_row == 0, -1.0, pltpu.roll(lower, COLS, 0))
    below = jnp.where(dev_row == ROWS - 1, -1.0, pltpu.roll(upper, DEV - COLS, 0))
    third = jnp.where(holder >= BLK // 2, above, below)
    out = jnp.full((DEV, BLK), -1.0, F32)
    for p, part in enumerate((upper, lower, third)):
        left = jnp.where(dev_col == 0, -1.0, pltpu.roll(part, 1, 0))
        right = jnp.where(dev_col == COLS - 1, -1.0, pltpu.roll(part, DEV - 1, 0))
        here = pltpu.roll(part, 4 * p, 1) if p else part
        out = jnp.where((lane >= 4 * p) & (lane < 4 * p + 3), here, out)
        out = jnp.where(lane == 4 * p + 3, pltpu.roll(left, 4 * p + 1, 1), out)
        out = jnp.where(lane == 12 + p, pltpu.roll(right, 12 + p, 1), out)
    return out


def owner_select(owner_ref, transpose):
    if transpose:
        return (owner_ref[0:1, :] == iota(0)).astype(BF)
    return (owner_ref[...].T == iota(1)).astype(BF)


def columns_of(slots, s):
    return jnp.broadcast_to(slots[:, s : s + 1], (DEV, BLK))


def pick_kernel(holder_ref, table_ref, ids_ref, owner_ref, out_ref, held_ref, stage):
    lane = iota(1)
    slots = slot_ids(ids_ref[...].astype(F32), holder_ref[0])
    cell = lane.astype(F32)
    held = dot(owner_select(owner_ref, False), table_ref[...]).astype(BF)
    held_ref[...] = held

    def pick(s):
        return dot((columns_of(slots, s) == cell).astype(BF), held)

    for p in range(3):
        for q in range(3):
            stage[pl.ds(4 * p + q, DEV, stride=SLOTS), :] = pick(4 * p + q)
        halo = jnp.where(lane >= BLK // 2, pick(4 * p + 3), pick(12 + p))
        stage[pl.ds(4 * p + 3, DEV, stride=SLOTS), :] = halo
    for s in range(12, SLOTS):
        stage[pl.ds(s, DEV, stride=SLOTS), :] = jnp.zeros((DEV, BLK), F32)
    out_ref[...] = stage[...].astype(BF)


def toeplitz(taps_ref, m, shift_stride=1):
    base = jnp.broadcast_to(taps_ref[pl.ds(m, 1), :], (BLK, 2 * BLK))
    return pltpu.roll(base, 0, 1, stride=1, stride_axis=0).astype(BF)


def litho_kernel(
    weights_ref, recv_ref, target_ref, row_ref, row_rev_ref, col_ref, col_rev_ref,
    out_ref, stage, wide, mask, columns_a, columns_b, field, light, grad, taps_a, taps_b, back_a, back_b,
):
    stage[...] = recv_ref[...].astype(F32)
    for q in range(4):
        for p in range(3):
            wide[p * BLK : (p + 1) * BLK, q * BLK : (q + 1) * BLK] = stage[
                pl.ds(4 * p + q, DEV, stride=SLOTS), :
            ]
    mask[...] = pltpu.roll(pltpu.roll(wide[...], HALF, 1), HALF, 0)[:EXT_R].astype(BF)
    for columns in (columns_a, columns_b):
        columns[:, EXT_R:, :] = jnp.zeros((2, 384 - EXT_R, TILE_C), BF)
    light[...] = jnp.zeros_like(light)

    def make_columns(k, columns):
        rolled = [toeplitz(col_rev_ref, 2 * k + r) for r in range(2)]
        col_matrix = jnp.concatenate(
            [
                jnp.concatenate([t[:, :BLK] for t in rolled], 1),
                jnp.concatenate([t[:, BLK:] for t in rolled], 1),
            ],
            0,
        )
        for q in range(3):
            made = dot(mask[:, q * BLK : (q + 2) * BLK], col_matrix).astype(BF)
            for r in range(2):
                columns[r, :EXT_R, q * BLK : (q + 1) * BLK] = made[:, r * BLK : (r + 1) * BLK]

    def make_field(k, columns):
        row_matrix = jnp.concatenate([toeplitz(row_ref, 2 * k + r) for r in range(2)], 1)
        weight = weights_ref[k // 2]
        for p in range(2):
            window = jnp.concatenate(
                [columns[r, p * BLK : (p + 2) * BLK, :] for r in range(2)], 0
            )
            made = dot(row_matrix, window)
            here = slice(p * BLK, (p + 1) * BLK)
            light[here] += weight * made * made
            field[k, here] = made

    make_columns(0, columns_a)

    def forward(i, carry):
        make_columns(2 * i + 1, columns_b)
        make_field(2 * i, columns_a)
        make_columns(jnp.minimum(2 * i + 2, CHAN - 1), columns_a)
        make_field(2 * i + 1, columns_b)
        return carry

    lax.fori_loop(0, CHAN // 2, forward, 0)
    resist = jax.nn.sigmoid(3.0 * (light[...] - 1.3))
    light[...] = 2.0 * (resist - target_ref[...]) * 3.0 * resist * (1.0 - resist)
    grad[...] = jnp.zeros_like(grad)
    for taps in (taps_a, taps_b):
        taps[...] = jnp.zeros_like(taps)

    def make_back(k, j, back):
        taps = (taps_a, taps_b)[j]
        weighted = (2.0 * weights_ref[k // 2] * field[k] * light[...]).astype(BF)
        for r in range(2):
            rolled = toeplitz(row_rev_ref, 2 * k + r)
            top, bottom = rolled[:, :BLK], rolled[:, BLK:]
            at = r * EXT_R
            taps[at : at + BLK, :BLK] = top
            taps[at + BLK : at + 2 * BLK, BLK:] = top
            taps[at + BLK : at + 2 * BLK, :BLK] = bottom
            taps[at + 2 * BLK : at + EXT_R, BLK:] = bottom[: EXT_R - 2 * BLK]
        made = dot(taps[...], weighted).astype(BF)
        for r in range(2):
            for q in range(3):
                at = (4 * q + 2 * j + r) * BLK
                back[:, at : at + BLK] = made[r * EXT_R : (r + 1) * EXT_R, q * BLK : (q + 1) * BLK]

    def add_grad(k, back):
        col_matrix = jnp.concatenate([toeplitz(col_ref, 2 * k + r) for r in range(4)], 0)
        for q in range(3):
            grad[:EXT_R, q * BLK : (q + 2) * BLK] += dot(
                back[:, 4 * q * BLK : 4 * (q + 1) * BLK], col_matrix
            )

    make_back(0, 0, back_a)
    make_back(1, 1, back_a)

    def backward(i, carry):
        k = 4 * i
        make_back(k + 2, 0, back_b)
        make_back(k + 3, 1, back_b)
        add_grad(k, back_a)
        later = jnp.minimum(k + 4, CHAN - 2)
        make_back(later, 0, back_a)
        make_back(later + 1, 1, back_a)
        add_grad(k + 2, back_b)
        return carry

    lax.fori_loop(0, CHAN // 4, backward, 0)
    wide[...] = pltpu.roll(pltpu.roll(grad[...], 384 - HALF, 0), 512 - HALF, 1)
    for q in range(4):
        for p in range(3):
            stage[pl.ds(4 * p + q, DEV, stride=SLOTS), :] = wide[
                p * BLK : (p + 1) * BLK, q * BLK : (q + 1) * BLK
            ]
    for s in range(12, SLOTS):
        stage[pl.ds(s, DEV, stride=SLOTS), :] = jnp.zeros((DEV, BLK), F32)
    out_ref[...] = stage[...].astype(BF)


def update_kernel(holder_ref, recv_ref, ids_ref, owner_ref, held_ref, out_ref, stage, out_stage):
    lane = iota(1)
    slots = slot_ids(ids_ref[...].astype(F32), holder_ref[0])
    slots_t = slots.T
    cell_down = iota(0).astype(F32)
    stage[...] = recv_ref[...].astype(F32)

    def gather(s, piece):
        select = (jnp.broadcast_to(slots_t[s : s + 1, :], (BLK, DEV)) == cell_down).astype(BF)
        return dot(select, stage[pl.ds(piece, DEV, stride=SLOTS), :].astype(BF))

    total = jnp.zeros((BLK, BLK), F32)
    from_left, from_right = total, total
    for p in range(3):
        for q in range(3):
            total += gather(4 * p + q, 4 * p + q)
        from_left += gather(4 * p + 3, 4 * p + 3)
        from_right += gather(12 + p, 4 * p + 3)
    total += jnp.where(lane >= BLK // 2, from_left, from_right)
    updated = (held_ref[...].astype(F32) - 0.05 * total).astype(BF)
    cell = lane.astype(F32)
    for p in range(2):
        for q in range(3):
            select = (columns_of(slots, 4 * p + q) == cell).astype(BF)
            out_stage[pl.ds(3 * p + q, DEV, stride=8), :] = dot(select, updated)
    by_owner = owner_select(owner_ref, True)
    out_stage[pl.ds(6, DEV, stride=8), :] = dot(by_owner, total.astype(BF))
    out_stage[pl.ds(7, DEV, stride=8), :] = jnp.zeros((DEV, BLK), F32)
    out_ref[...] = out_stage[...].astype(BF)


def unpack_kernel(recv_ref, grad_ref, mask_ref, stage):
    stage[...] = recv_ref[...].astype(F32)
    for p in range(2):
        for q in range(3):
            mask_ref[p * BLK : (p + 1) * BLK, q * BLK : (q + 1) * BLK] = stage[
                pl.ds(3 * p + q, DEV, stride=8), :
            ]
    grad_ref[...] = stage[pl.ds(6, DEV, stride=8), :]


SMEM = pl.BlockSpec(memory_space=pltpu.SMEM)
VMEM = pl.BlockSpec(memory_space=pltpu.VMEM)


def call(kernel, out_shape, in_specs, scratch, name):
    return pl.pallas_call(
        kernel,
        out_shape=out_shape,
        in_specs=in_specs,
        out_specs=jax.tree.map(lambda _: VMEM, out_shape),
        scratch_shapes=scratch,
        name=name,
    )


def exchange(x):
    return lax.all_to_all(x, AXES, 0, 0, tiled=True)


def per_device(cells, target, row_taps, col_taps, socs, cell_of_block, owner_map):
    struct = jax.ShapeDtypeStruct
    holder = (lax.axis_index("row") * COLS + lax.axis_index("col")).astype(jnp.int32).reshape(1)
    weights = socs / jnp.sum(socs)
    owner = jnp.broadcast_to(owner_map[None, :], (DEV, DEV))

    def spread(taps, reverse):
        flat = taps.reshape(2 * CHAN, 2 * HALF + 1).astype(F32)
        gap = jnp.zeros((2 * CHAN, 2 * BLK - 2 * HALF - 1), F32)
        if reverse:
            return jnp.concatenate([flat[:, :1], gap, flat[:, :0:-1]], 1)
        return jnp.concatenate([flat, gap], 1)

    own_ids = jnp.pad(cell_of_block.reshape(1, 6).astype(BF), ((0, 0), (0, BLK - 6)))
    first = jnp.stack([cells[0].astype(BF), jnp.broadcast_to(own_ids, (BLK, BLK))], 1)
    first = exchange(first)
    table, ids = first[:, 0], first[:, 1]

    picked, held = call(
        pick_kernel,
        (struct((DEV * SLOTS, BLK), BF), struct((BLK, BLK), BF)),
        [SMEM, VMEM, VMEM, VMEM],
        [pltpu.VMEM((DEV * SLOTS, BLK), F32)],
        "pick",
    )(holder, table, ids, owner)
    received = exchange(picked.reshape(DEV, SLOTS, BLK)).reshape(DEV * SLOTS, BLK)

    pieces = call(
        litho_kernel,
        struct((DEV * SLOTS, BLK), BF),
        [SMEM] + [VMEM] * 6,
        [
            pltpu.VMEM((DEV * SLOTS, BLK), F32),
            pltpu.VMEM((384, 512), F32),
            pltpu.VMEM((EXT_R, 512), BF),
            pltpu.VMEM((2, 384, TILE_C), BF),
            pltpu.VMEM((2, 384, TILE_C), BF),
            pltpu.VMEM((CHAN, TILE_R, TILE_C), F32),
            pltpu.VMEM((TILE_R, TILE_C), F32),
            pltpu.VMEM((384, 512), F32),
            pltpu.VMEM((2 * EXT_R, TILE_R), BF),
            pltpu.VMEM((2 * EXT_R, TILE_R), BF),
            pltpu.VMEM((EXT_R, 12 * BLK), BF),
            pltpu.VMEM((EXT_R, 12 * BLK), BF),
        ],
        "litho",
    )(
        weights, received, target,
        spread(row_taps, False), spread(row_taps, True),
        spread(col_taps, False), spread(col_taps, True),
    )
    pieces = exchange(pieces.reshape(DEV, SLOTS, BLK)).reshape(DEV * SLOTS, BLK)

    results = call(
        update_kernel,
        struct((DEV * 8, BLK), BF),
        [SMEM] + [VMEM] * 4,
        [pltpu.VMEM((DEV * SLOTS, BLK), F32), pltpu.VMEM((DEV * 8, BLK), F32)],
        "update",
    )(holder, pieces, ids, owner, held)
    results = exchange(results.reshape(DEV, 8, BLK)).reshape(DEV * 8, BLK)

    gradient, new_mask = call(
        unpack_kernel,
        (struct((BLK, BLK), F32), struct((TILE_R, TILE_C), F32)),
        [VMEM],
        [pltpu.VMEM((DEV * 8, BLK), F32)],
        "unpack",
    )(results)
    return gradient.reshape(1, BLK, BLK), new_mask


def solution(mesh):
    in_specs = (P(AXES, None, None), P("row", "col"), P(), P(), P(), P("row", "col"), P())
    out_specs = (P(AXES, None, None), P("row", "col"))
    return jax.shard_map(
        per_device, mesh=mesh, in_specs=in_specs, out_specs=out_specs, check_vma=False
    )
```

```python
import jax
import jax.numpy as jnp
from jax import lax
from jax.experimental import pallas as pl
from jax.experimental.pallas import tpu as pltpu
from jax.sharding import PartitionSpec as P

AXES = ("row", "col")
ROWS, COLS = 4, 32
DEV = ROWS * COLS
BLK = 128
HALF = 17
WIN = BLK + 2 * HALF
TILE_R, TILE_C = 256, 384
EXT_R = 296
TAIL = 48
CHAN = 24
SLOTS = 16
PER_COL = 12 * ROWS
BF, F32 = jnp.bfloat16, jnp.float32


def dot(a, b):
    return lax.dot_general(a, b, (((1,), (0,)), ((), ())), preferred_element_type=F32)


def iota(dim, shape=(DEV, BLK)):
    return lax.broadcasted_iota(jnp.int32, shape, dim)


def slot_ids(ids, holder_col):
    lane, dev = iota(1), iota(0)
    dev_row, dev_col = dev // COLS, dev % COLS
    upper = ids
    lower = pltpu.roll(ids, BLK - 3, 1)
    above = jnp.where(dev_row == 0, -1.0, pltpu.roll(lower, COLS, 0))
    below = jnp.where(dev_row == ROWS - 1, -1.0, pltpu.roll(upper, DEV - COLS, 0))
    third = jnp.where(holder_col >= COLS // 2, above, below)
    out = jnp.full((DEV, BLK), -1.0, F32)
    for p, part in enumerate((upper, lower, third)):
        left = jnp.where(dev_col == 0, -1.0, pltpu.roll(part, 1, 0))
        right = jnp.where(dev_col == COLS - 1, -1.0, pltpu.roll(part, DEV - 1, 0))
        here = pltpu.roll(part, 4 * p, 1) if p else part
        out = jnp.where((lane >= 4 * p) & (lane < 4 * p + 3), here, out)
        out = jnp.where(lane == 4 * p + 3, pltpu.roll(left, 4 * p + 1, 1), out)
        out = jnp.where(lane == 12 + p, pltpu.roll(right, 12 + p, 1), out)
    return out


def owner_select(owner_ref, transpose):
    owner = jnp.broadcast_to(owner_ref[...], (DEV, DEV))
    if transpose:
        return (owner == iota(0)).astype(BF)
    return (owner.astype(F32).T == iota(1).astype(F32)).astype(BF)


def columns_of(slots, s):
    return jnp.broadcast_to(slots[:, s : s + 1], (slots.shape[0], BLK))


def pack_kernel(blocks_ref, cells_ref, out_ref, stage):
    lane = iota(1, (COLS, BLK))
    ids = jnp.full((COLS, BLK), -1.0, F32)
    for n in range(6):
        ids = jnp.where(lane == n, blocks_ref[n // 3, n % 3].astype(F32), ids)
    for s in range(ROWS):
        stage[pl.ds(s, COLS, stride=8), :] = cells_ref[pl.ds(s, COLS, stride=ROWS), :]
    stage[pl.ds(ROWS, COLS, stride=8), :] = ids
    for s in range(ROWS + 1, 8):
        stage[pl.ds(s, COLS, stride=8), :] = jnp.zeros((COLS, BLK), F32)
    packed = stage[...].astype(BF)
    for r in range(ROWS):
        out_ref[r * COLS * 8 : (r + 1) * COLS * 8, :] = packed


def pick_kernel(place_ref, first_ref, owner_ref, out_ref, held_ref, slots_ref, stage, mine, out_stage):
    stage[...] = first_ref[...].astype(F32)
    slots = slot_ids(stage[pl.ds(ROWS, DEV, stride=8), :], place_ref[1])
    slots_ref[...] = slots
    table = jnp.concatenate([stage[pl.ds(s, DEV, stride=8), :] for s in range(ROWS)], 1)
    held = dot(owner_select(owner_ref, False), table.astype(BF)).astype(BF)
    row = place_ref[0]
    own = held[:, :BLK].astype(F32)
    for s in range(1, ROWS):
        own = jnp.where(row == s, held[:, s * BLK : (s + 1) * BLK].astype(F32), own)
    held_ref[...] = own
    mine[...] = slots_ref[pl.ds(pl.multiple_of(row * COLS, COLS), COLS), :]
    here = mine[...]
    cell = iota(1, (COLS, BLK)).astype(F32)
    select = jnp.concatenate([(columns_of(here, s) == cell).astype(BF) for s in range(15)], 0)
    picked = dot(select, held)
    wide_lane = iota(1, (COLS, ROWS * BLK)) % BLK
    for t in range(12):
        made = picked[t * COLS : (t + 1) * COLS]
        if t % 4 == 3:
            at = (12 + t // 4) * COLS
            made = jnp.where(wide_lane >= BLK // 2, made, picked[at : at + COLS])
        for s in range(ROWS):
            out_stage[pl.ds(ROWS * t + s, COLS, stride=PER_COL), :] = made[:, s * BLK : (s + 1) * BLK]
    out_ref[...] = out_stage[...].astype(BF)


def toeplitz(taps_ref, m):
    base = jnp.broadcast_to(taps_ref[pl.ds(m, 1), :], (BLK, 2 * BLK))
    return pltpu.roll(base, 0, 1, stride=1, stride_axis=0).astype(BF)


def litho_kernel(
    weights_ref, recv_ref, target_ref, row_ref, row_rev_ref, col_ref, col_rev_ref,
    out_ref, stage, wide, mask, columns_a, columns_b, field, light, grad, back_a, back_b,
):
    stage[: COLS * PER_COL, :] = recv_ref[...].astype(F32)
    for q in range(4):
        for p in range(3):
            for s in range(ROWS):
                wide[q, pl.ds(p * BLK + s, COLS, stride=ROWS), :] = stage[
                    pl.ds(ROWS * (4 * p + q) + s, COLS, stride=PER_COL), :
                ]
    whole = jnp.concatenate([wide[q] for q in range(4)], 1)
    mask[...] = pltpu.roll(pltpu.roll(whole, HALF, 1), HALF, 0)[:EXT_R].astype(BF)
    for columns in (columns_a, columns_b):
        columns[:, EXT_R:, :] = jnp.zeros((2, 384 - EXT_R, TILE_C), BF)
    light[...] = jnp.zeros_like(light)

    def make_columns(k, columns):
        rolled = [toeplitz(col_rev_ref, 2 * k + r) for r in range(2)]
        col_matrix = jnp.concatenate(
            [
                jnp.concatenate([t[:, :BLK] for t in rolled], 1),
                jnp.concatenate([t[:, BLK:] for t in rolled], 1),
            ],
            0,
        )
        for q in range(3):
            made = dot(mask[:, q * BLK : (q + 2) * BLK], col_matrix).astype(BF)
            for r in range(2):
                columns[r, :EXT_R, q * BLK : (q + 1) * BLK] = made[:, r * BLK : (r + 1) * BLK]

    def make_field(k, columns):
        row_matrix = jnp.concatenate([toeplitz(row_ref, 2 * k + r) for r in range(2)], 1)
        weight = weights_ref[k // 2]
        windows = [
            jnp.concatenate([columns[r, p * BLK : (p + 2) * BLK, :] for r in range(2)], 0)
            for p in range(2)
        ]
        last = dot(row_matrix, jnp.concatenate([w[:, 2 * BLK :] for w in windows], 1))
        for p in range(2):
            made = jnp.concatenate(
                [dot(row_matrix, windows[p][:, : 2 * BLK]), last[:, p * BLK : (p + 1) * BLK]], 1
            )
            here = slice(p * BLK, (p + 1) * BLK)
            light[here] += weight * made * made
            field[k, here] = made

    make_columns(0, columns_a)

    def forward(i, carry):
        make_columns(2 * i + 1, columns_b)
        make_field(2 * i, columns_a)
        make_columns(jnp.minimum(2 * i + 2, CHAN - 1), columns_a)
        make_field(2 * i + 1, columns_b)
        return carry

    lax.fori_loop(0, CHAN // 2, forward, 0)
    resist = jax.nn.sigmoid(3.0 * (light[...] - 1.3))
    light[...] = 2.0 * (resist - target_ref[...]) * 3.0 * resist * (1.0 - resist)
    grad[...] = jnp.zeros_like(grad)

    def make_back(k, j, back):
        weight = 2.0 * weights_ref[k // 2]
        upper, lower = [
            (weight * field[k, p * BLK : (p + 1) * BLK] * light[p * BLK : (p + 1) * BLK]).astype(BF)
            for p in range(2)
        ]
        rolled = [toeplitz(row_rev_ref, 2 * k + r) for r in range(2)]
        both = jnp.concatenate(rolled, 0)
        tail = jnp.concatenate([t[:TAIL, BLK:] for t in rolled], 0)
        second = jnp.concatenate([lower, upper], 0)
        first = jnp.concatenate([upper, jnp.zeros_like(upper)], 0)
        last = dot(both, jnp.concatenate([first[:, 2 * BLK :], second[:, 2 * BLK :]], 1)).astype(BF)
        parts = [
            dot(both[:, :BLK], upper[:, : 2 * BLK]).astype(BF),
            dot(both, second[:, : 2 * BLK]).astype(BF),
        ]
        end = dot(tail, lower).astype(BF)
        for r in range(2):
            for q in range(3):
                at = (4 * q + 2 * j + r) * BLK
                for p in range(2):
                    piece = last if q == 2 else parts[p]
                    lanes = p * BLK if q == 2 else q * BLK
                    back[p * BLK : (p + 1) * BLK, at : at + BLK] = piece[
                        r * BLK : (r + 1) * BLK, lanes : lanes + BLK
                    ]
                back[2 * BLK :, at : at + BLK] = end[
                    r * TAIL : r * TAIL + EXT_R - 2 * BLK, q * BLK : (q + 1) * BLK
                ]

    def add_grad(k, back):
        col_matrix = jnp.concatenate([toeplitz(col_ref, 2 * k + r) for r in range(4)], 0)
        for q in range(3):
            grad[:EXT_R, q * BLK : (q + 2) * BLK] += dot(
                back[:, 4 * q * BLK : 4 * (q + 1) * BLK], col_matrix
            )

    make_back(0, 0, back_a)
    make_back(1, 1, back_a)

    def backward(i, carry):
        k = 4 * i
        make_back(k + 2, 0, back_b)
        make_back(k + 3, 1, back_b)
        add_grad(k, back_a)
        later = jnp.minimum(k + 4, CHAN - 2)
        make_back(later, 0, back_a)
        make_back(later + 1, 1, back_a)
        add_grad(k + 2, back_b)
        return carry

    lax.fori_loop(0, CHAN // 4, backward, 0)
    whole = pltpu.roll(pltpu.roll(grad[...], 384 - HALF, 0), 512 - HALF, 1)
    for q in range(4):
        wide[q] = whole[:, q * BLK : (q + 1) * BLK]
    for q in range(4):
        for p in range(3):
            for r in range(ROWS):
                stage[pl.ds(r * COLS * SLOTS + 4 * p + q, COLS, stride=SLOTS), :] = wide[
                    q, pl.ds(p * BLK + r, COLS, stride=ROWS), :
                ]
    for s in range(12, SLOTS):
        stage[pl.ds(s, DEV, stride=SLOTS), :] = jnp.zeros((DEV, BLK), F32)
    out_ref[...] = stage[...].astype(BF)


def update_kernel(recv_ref, slots_ref, owner_ref, held_ref, out_ref, stage, out_stage):
    lane = iota(1)
    slots = slots_ref[...]
    slots_t = slots.T
    cell_down = iota(0).astype(F32)
    stage[...] = recv_ref[...].astype(F32)

    def gather(s, piece):
        select = (jnp.broadcast_to(slots_t[s : s + 1, :], (BLK, DEV)) == cell_down).astype(BF)
        return dot(select, stage[pl.ds(piece, DEV, stride=SLOTS), :].astype(BF))

    total = jnp.zeros((BLK, BLK), F32)
    from_left, from_right = total, total
    for p in range(3):
        for q in range(3):
            total += gather(4 * p + q, 4 * p + q)
        from_left += gather(4 * p + 3, 4 * p + 3)
        from_right += gather(12 + p, 4 * p + 3)
    total += jnp.where(lane >= BLK // 2, from_left, from_right)
    updated = (held_ref[...] - 0.05 * total).astype(BF)
    cell = lane.astype(F32)
    for p in range(2):
        for q in range(3):
            select = (columns_of(slots, 4 * p + q) == cell).astype(BF)
            out_stage[pl.ds(3 * p + q, DEV, stride=8), :] = dot(select, updated)
    by_owner = owner_select(owner_ref, True)
    out_stage[pl.ds(6, DEV, stride=8), :] = dot(by_owner, total.astype(BF))
    out_stage[pl.ds(7, DEV, stride=8), :] = jnp.zeros((DEV, BLK), F32)
    out_ref[...] = out_stage[...].astype(BF)


def unpack_kernel(recv_ref, grad_ref, mask_ref, stage, wide):
    stage[...] = recv_ref[...].astype(F32)
    for r in range(ROWS):
        for p in range(2):
            for q in range(3):
                wide[q, pl.ds(p * BLK + r, COLS, stride=ROWS), :] = stage[
                    pl.ds(r * COLS * 8 + 3 * p + q, COLS, stride=8), :
                ]
        grad_ref[pl.ds(r, COLS, stride=ROWS), :] = stage[pl.ds(r * COLS * 8 + 6, COLS, stride=8), :]
    for q in range(3):
        mask_ref[:, q * BLK : (q + 1) * BLK] = wide[q]


SMEM = pl.BlockSpec(memory_space=pltpu.SMEM)
VMEM = pl.BlockSpec(memory_space=pltpu.VMEM)


def call(kernel, out_shape, in_specs, scratch, name, limit=8):
    return pl.pallas_call(
        kernel,
        out_shape=out_shape,
        in_specs=in_specs,
        out_specs=jax.tree.map(lambda _: VMEM, out_shape),
        scratch_shapes=scratch,
        name=name,
        compiler_params=pltpu.CompilerParams(vmem_limit_bytes=limit << 20),
    )


def exchange(x, axes=AXES):
    return lax.all_to_all(x, axes, 0, 0, tiled=True)


def per_device(cells, target, row_taps, col_taps, socs, cell_of_block, owner_map):
    struct = jax.ShapeDtypeStruct
    place = jnp.stack([lax.axis_index("row"), lax.axis_index("col")]).astype(jnp.int32)
    weights = socs / jnp.sum(socs)
    owner = owner_map.reshape(1, DEV)

    def spread(taps, reverse):
        flat = taps.reshape(2 * CHAN, 2 * HALF + 1).astype(F32)
        gap = jnp.zeros((2 * CHAN, 2 * BLK - 2 * HALF - 1), F32)
        if reverse:
            return jnp.concatenate([flat[:, :1], gap, flat[:, :0:-1]], 1)
        return jnp.concatenate([flat, gap], 1)

    first = call(
        pack_kernel,
        struct((DEV * 8, BLK), BF),
        [SMEM, VMEM],
        [pltpu.VMEM((COLS * 8, BLK), F32)],
        "pack",
    )(cell_of_block, cells.reshape(BLK, BLK))
    first = exchange(first.reshape(DEV, 8, BLK)).reshape(DEV * 8, BLK)

    picked, held, slots = call(
        pick_kernel,
        (struct((COLS * PER_COL, BLK), BF), struct((BLK, BLK), F32), struct((DEV, BLK), F32)),
        [SMEM, VMEM, VMEM],
        [
            pltpu.VMEM((DEV * 8, BLK), F32),
            pltpu.VMEM((COLS, BLK), F32),
            pltpu.VMEM((COLS * PER_COL, BLK), F32),
        ],
        "pick",
    )(place, first, owner)
    received = exchange(picked.reshape(COLS, PER_COL, BLK), "col").reshape(COLS * PER_COL, BLK)

    pieces = call(
        litho_kernel,
        struct((DEV * SLOTS, BLK), BF),
        [SMEM] + [VMEM] * 6,
        [
            pltpu.VMEM((DEV * SLOTS, BLK), F32),
            pltpu.VMEM((4, 384, BLK), F32),
            pltpu.VMEM((EXT_R, 512), BF),
            pltpu.VMEM((2, 384, TILE_C), BF),
            pltpu.VMEM((2, 384, TILE_C), BF),
            pltpu.VMEM((CHAN, TILE_R, TILE_C), F32),
            pltpu.VMEM((TILE_R, TILE_C), F32),
            pltpu.VMEM((384, 512), F32),
            pltpu.VMEM((EXT_R, 12 * BLK), BF),
            pltpu.VMEM((EXT_R, 12 * BLK), BF),
        ],
        "litho",
        32,
    )(
        weights, received, target,
        spread(row_taps, False), spread(row_taps, True),
        spread(col_taps, False), spread(col_taps, True),
    )
    pieces = exchange(pieces.reshape(DEV, SLOTS, BLK)).reshape(DEV * SLOTS, BLK)

    results = call(
        update_kernel,
        struct((DEV * 8, BLK), BF),
        [VMEM] * 4,
        [pltpu.VMEM((DEV * SLOTS, BLK), F32), pltpu.VMEM((DEV * 8, BLK), F32)],
        "update",
    )(pieces, slots, owner, held)
    results = exchange(results.reshape(DEV, 8, BLK)).reshape(DEV * 8, BLK)

    gradient, new_mask = call(
        unpack_kernel,
        (struct((BLK, BLK), F32), struct((TILE_R, TILE_C), F32)),
        [VMEM],
        [pltpu.VMEM((DEV * 8, BLK), F32), pltpu.VMEM((3, TILE_R, BLK), F32)],
        "unpack",
    )(results)
    return gradient.reshape(1, BLK, BLK), new_mask


def solution(mesh):
    in_specs = (P(AXES, None, None), P("row", "col"), P(), P(), P(), P("row", "col"), P())
    out_specs = (P(AXES, None, None), P("row", "col"))
    return jax.shard_map(
        per_device, mesh=mesh, in_specs=in_specs, out_specs=out_specs, check_vma=False
    )
```

```python
import jax
import jax.numpy as jnp
from jax import lax
from jax.experimental import pallas as pl
from jax.experimental.pallas import tpu as pltpu
from jax.sharding import PartitionSpec as P

AXES = ("row", "col")
ROWS, COLS = 4, 32
DEV = ROWS * COLS
BLK = 128
HALF = 17
WIN = BLK + 2 * HALF
TILE_R, TILE_C = 256, 384
EXT_R = 296
TAIL = 48
CHAN = 24
SLOTS = 16
PER_COL = 12 * ROWS
BF, F32 = jnp.bfloat16, jnp.float32


def dot(a, b):
    return lax.dot_general(a, b, (((1,), (0,)), ((), ())), preferred_element_type=F32)


def iota(dim, shape=(DEV, BLK)):
    return lax.broadcasted_iota(jnp.int32, shape, dim)


def slot_ids(ids, holder_col):
    lane, dev = iota(1), iota(0)
    dev_row, dev_col = dev // COLS, dev % COLS
    upper = ids
    lower = pltpu.roll(ids, BLK - 3, 1)
    above = jnp.where(dev_row == 0, -1.0, pltpu.roll(lower, COLS, 0))
    below = jnp.where(dev_row == ROWS - 1, -1.0, pltpu.roll(upper, DEV - COLS, 0))
    third = jnp.where(holder_col >= COLS // 2, above, below)
    out = jnp.full((DEV, BLK), -1.0, F32)
    for p, part in enumerate((upper, lower, third)):
        left = jnp.where(dev_col == 0, -1.0, pltpu.roll(part, 1, 0))
        right = jnp.where(dev_col == COLS - 1, -1.0, pltpu.roll(part, DEV - 1, 0))
        here = pltpu.roll(part, 4 * p, 1) if p else part
        out = jnp.where((lane >= 4 * p) & (lane < 4 * p + 3), here, out)
        out = jnp.where(lane == 4 * p + 3, pltpu.roll(left, 4 * p + 1, 1), out)
        out = jnp.where(lane == 12 + p, pltpu.roll(right, 12 + p, 1), out)
    return out


def owner_select(owner_ref, transpose):
    owner = jnp.broadcast_to(owner_ref[...], (DEV, DEV))
    if transpose:
        return (owner == iota(0)).astype(BF)
    return (owner.astype(F32).T == iota(1).astype(F32)).astype(BF)


def columns_of(slots, s):
    return jnp.broadcast_to(slots[:, s : s + 1], (slots.shape[0], BLK))


def pack_kernel(blocks_hbm, cells_hbm, out_hbm, blocks_ref, cells, stage, packed, ids_sem, in_sem, out_sem):
    fetch_ids = pltpu.make_async_copy(blocks_hbm, blocks_ref, ids_sem)
    fetch_ids.start()
    fetch = pltpu.make_async_copy(cells_hbm, cells, in_sem)
    fetch.start()
    lane = iota(1, (COLS, BLK))
    ids = jnp.full((COLS, BLK), -1.0, F32)
    for s in range(ROWS + 1, 8):
        stage[pl.ds(s, COLS, stride=8), :] = jnp.zeros((COLS, BLK), F32)
    fetch_ids.wait()
    for n in range(6):
        ids = jnp.where(lane == n, blocks_ref[n // 3, n % 3].astype(F32), ids)
    stage[pl.ds(ROWS, COLS, stride=8), :] = ids
    fetch.wait()
    for s in range(ROWS):
        stage[pl.ds(s, COLS, stride=8), :] = cells[pl.ds(s, COLS, stride=ROWS), :]
    packed[...] = stage[...].astype(BF)
    copies = [
        pltpu.make_async_copy(packed, out_hbm.at[pl.ds(r * COLS * 8, COLS * 8)], out_sem.at[r])
        for r in range(ROWS)
    ]
    for copy in copies:
        copy.start()
    for copy in copies:
        copy.wait()


def pick_kernel(
    place_ref, first_ref, owner_hbm, out_ref, held_ref, slots_ref, by_owner_ref,
    owner_ref, stage, mine, out_stage, sem,
):
    fetch = pltpu.make_async_copy(owner_hbm, owner_ref, sem)
    fetch.start()
    stage[...] = first_ref[...].astype(F32)
    slots = slot_ids(stage[pl.ds(ROWS, DEV, stride=8), :], place_ref[1])
    slots_ref[...] = slots
    table = jnp.concatenate([stage[pl.ds(s, DEV, stride=8), :] for s in range(ROWS)], 1)
    fetch.wait()
    by_owner_ref[...] = owner_select(owner_ref, True)
    held = dot(owner_select(owner_ref, False), table.astype(BF)).astype(BF)
    row = place_ref[0]
    own = held[:, :BLK].astype(F32)
    for s in range(1, ROWS):
        own = jnp.where(row == s, held[:, s * BLK : (s + 1) * BLK].astype(F32), own)
    held_ref[...] = own
    mine[...] = slots_ref[pl.ds(pl.multiple_of(row * COLS, COLS), COLS), :]
    here = mine[...]
    cell = iota(1, (COLS, BLK)).astype(F32)
    select = jnp.concatenate([(columns_of(here, s) == cell).astype(BF) for s in range(15)], 0)
    picked = dot(select, held)
    wide_lane = iota(1, (COLS, ROWS * BLK)) % BLK
    for t in range(12):
        made = picked[t * COLS : (t + 1) * COLS]
        if t % 4 == 3:
            at = (12 + t // 4) * COLS
            made = jnp.where(wide_lane >= BLK // 2, made, picked[at : at + COLS])
        for s in range(ROWS):
            out_stage[pl.ds(ROWS * t + s, COLS, stride=PER_COL), :] = made[:, s * BLK : (s + 1) * BLK]
    out_ref[...] = out_stage[...].astype(BF)


def toeplitz(taps_ref, m):
    base = jnp.broadcast_to(taps_ref[pl.ds(m, 1), :], (BLK, 2 * BLK))
    return pltpu.roll(base, 0, 1, stride=1, stride_axis=0).astype(BF)


def litho_kernel(
    weights_ref, recv_ref, target_ref, row_ref, row_rev_ref, col_ref, col_rev_ref,
    out_ref, stage, wide, mask, columns_a, columns_b, field, light, grad, back_a, back_b,
):
    stage[: COLS * PER_COL, :] = recv_ref[...].astype(F32)
    for q in range(4):
        for p in range(3):
            for s in range(ROWS):
                wide[q, pl.ds(p * BLK + s, COLS, stride=ROWS), :] = stage[
                    pl.ds(ROWS * (4 * p + q) + s, COLS, stride=PER_COL), :
                ]
    whole = jnp.concatenate([wide[q] for q in range(4)], 1)
    mask[...] = pltpu.roll(pltpu.roll(whole, HALF, 1), HALF, 0)[:EXT_R].astype(BF)
    for columns in (columns_a, columns_b):
        columns[:, EXT_R:, :] = jnp.zeros((2, 384 - EXT_R, TILE_C), BF)
    light[...] = jnp.zeros_like(light)

    def make_columns(k, columns):
        rolled = [toeplitz(col_rev_ref, 2 * k + r) for r in range(2)]
        col_matrix = jnp.concatenate(
            [
                jnp.concatenate([t[:, :BLK] for t in rolled], 1),
                jnp.concatenate([t[:, BLK:] for t in rolled], 1),
            ],
            0,
        )
        for q in range(3):
            made = dot(mask[:, q * BLK : (q + 2) * BLK], col_matrix).astype(BF)
            for r in range(2):
                columns[r, :EXT_R, q * BLK : (q + 1) * BLK] = made[:, r * BLK : (r + 1) * BLK]

    def make_field(k, columns):
        row_matrix = jnp.concatenate([toeplitz(row_ref, 2 * k + r) for r in range(2)], 1)
        weight = weights_ref[k // 2]
        windows = [
            jnp.concatenate([columns[r, p * BLK : (p + 2) * BLK, :] for r in range(2)], 0)
            for p in range(2)
        ]
        last = dot(row_matrix, jnp.concatenate([w[:, 2 * BLK :] for w in windows], 1))
        for p in range(2):
            made = jnp.concatenate(
                [dot(row_matrix, windows[p][:, : 2 * BLK]), last[:, p * BLK : (p + 1) * BLK]], 1
            )
            here = slice(p * BLK, (p + 1) * BLK)
            light[here] += weight * made * made
            field[k, here] = made

    make_columns(0, columns_a)

    buffers = (columns_a, columns_b)
    for k in range(CHAN):
        if k + 1 < CHAN:
            make_columns(k + 1, buffers[(k + 1) % 2])
        make_field(k, buffers[k % 2])
    resist = jax.nn.sigmoid(3.0 * (light[...] - 1.3))
    light[...] = 2.0 * (resist - target_ref[...]) * 3.0 * resist * (1.0 - resist)
    grad[...] = jnp.zeros_like(grad)

    def make_back(k, j, back):
        weight = 2.0 * weights_ref[k // 2]
        upper, lower = [
            (weight * field[k, p * BLK : (p + 1) * BLK] * light[p * BLK : (p + 1) * BLK]).astype(BF)
            for p in range(2)
        ]
        rolled = [toeplitz(row_rev_ref, 2 * k + r) for r in range(2)]
        both = jnp.concatenate(rolled, 0)
        tail = jnp.concatenate([t[:TAIL, BLK:] for t in rolled], 0)
        second = jnp.concatenate([lower, upper], 0)
        first = jnp.concatenate([upper, jnp.zeros_like(upper)], 0)
        last = dot(both, jnp.concatenate([first[:, 2 * BLK :], second[:, 2 * BLK :]], 1)).astype(BF)
        parts = [
            dot(both[:, :BLK], upper[:, : 2 * BLK]).astype(BF),
            dot(both, second[:, : 2 * BLK]).astype(BF),
        ]
        end = dot(tail, lower).astype(BF)
        for r in range(2):
            for q in range(3):
                at = (4 * q + 2 * j + r) * BLK
                for p in range(2):
                    piece = last if q == 2 else parts[p]
                    lanes = p * BLK if q == 2 else q * BLK
                    back[p * BLK : (p + 1) * BLK, at : at + BLK] = piece[
                        r * BLK : (r + 1) * BLK, lanes : lanes + BLK
                    ]
                back[2 * BLK :, at : at + BLK] = end[
                    r * TAIL : r * TAIL + EXT_R - 2 * BLK, q * BLK : (q + 1) * BLK
                ]

    def add_grad(k, back):
        col_matrix = jnp.concatenate([toeplitz(col_ref, 2 * k + r) for r in range(4)], 0)
        for q in range(3):
            grad[:EXT_R, q * BLK : (q + 2) * BLK] += dot(
                back[:, 4 * q * BLK : 4 * (q + 1) * BLK], col_matrix
            )

    backs = (back_a, back_b)
    for j in range(2):
        make_back(j, j, back_a)
    for n in range(CHAN // 2):
        if n + 1 < CHAN // 2:
            for j in range(2):
                make_back(2 * n + 2 + j, j, backs[(n + 1) % 2])
        add_grad(2 * n, backs[n % 2])
    whole = pltpu.roll(pltpu.roll(grad[...], 384 - HALF, 0), 512 - HALF, 1)
    for q in range(4):
        wide[q] = whole[:, q * BLK : (q + 1) * BLK]
    for q in range(4):
        for p in range(3):
            for r in range(ROWS):
                stage[pl.ds(r * COLS * SLOTS + 4 * p + q, COLS, stride=SLOTS), :] = wide[
                    q, pl.ds(p * BLK + r, COLS, stride=ROWS), :
                ]
    for s in range(12, SLOTS):
        stage[pl.ds(s, DEV, stride=SLOTS), :] = jnp.zeros((DEV, BLK), F32)
    out_ref[...] = stage[...].astype(BF)


def update_kernel(recv_ref, slots_ref, by_owner_ref, held_ref, out_ref, stage, out_stage):
    lane = iota(1)
    slots = slots_ref[...]
    slots_t = slots.T
    cell_down = iota(0).astype(F32)
    stage[...] = recv_ref[...].astype(F32)

    def gather(s, piece):
        select = (jnp.broadcast_to(slots_t[s : s + 1, :], (BLK, DEV)) == cell_down).astype(BF)
        return dot(select, stage[pl.ds(piece, DEV, stride=SLOTS), :].astype(BF))

    total = jnp.zeros((BLK, BLK), F32)
    from_left, from_right = total, total
    for p in range(3):
        for q in range(3):
            total += gather(4 * p + q, 4 * p + q)
        from_left += gather(4 * p + 3, 4 * p + 3)
        from_right += gather(12 + p, 4 * p + 3)
    total += jnp.where(lane >= BLK // 2, from_left, from_right)
    updated = (held_ref[...] - 0.05 * total).astype(BF)
    cell = lane.astype(F32)
    for p in range(2):
        for q in range(3):
            select = (columns_of(slots, 4 * p + q) == cell).astype(BF)
            out_stage[pl.ds(3 * p + q, DEV, stride=8), :] = dot(select, updated)
    out_stage[pl.ds(6, DEV, stride=8), :] = dot(by_owner_ref[...], total.astype(BF))
    out_stage[pl.ds(7, DEV, stride=8), :] = jnp.zeros((DEV, BLK), F32)
    out_ref[...] = out_stage[...].astype(BF)


def unpack_kernel(recv_ref, grad_ref, mask_ref, stage, wide):
    stage[...] = recv_ref[...].astype(F32)
    for r in range(ROWS):
        for p in range(2):
            for q in range(3):
                wide[q, pl.ds(p * BLK + r, COLS, stride=ROWS), :] = stage[
                    pl.ds(r * COLS * 8 + 3 * p + q, COLS, stride=8), :
                ]
        grad_ref[pl.ds(r, COLS, stride=ROWS), :] = stage[pl.ds(r * COLS * 8 + 6, COLS, stride=8), :]
    for q in range(3):
        mask_ref[:, q * BLK : (q + 1) * BLK] = wide[q]


SMEM = pl.BlockSpec(memory_space=pltpu.SMEM)
VMEM = pl.BlockSpec(memory_space=pltpu.VMEM)
HBM = pl.BlockSpec(memory_space=pltpu.HBM)


def call(kernel, out_shape, in_specs, scratch, name, limit=8, out_space=VMEM):
    return pl.pallas_call(
        kernel,
        out_shape=out_shape,
        in_specs=in_specs,
        out_specs=jax.tree.map(lambda _: out_space, out_shape),
        scratch_shapes=scratch,
        name=name,
        compiler_params=pltpu.CompilerParams(vmem_limit_bytes=limit << 20),
    )


def in_hbm(x):
    return pltpu.with_memory_space_constraint(x, pltpu.HBM)


def exchange(x, axes=AXES):
    return lax.all_to_all(x, axes, 0, 0, tiled=True)


def per_device(cells, target, row_taps, col_taps, socs, cell_of_block, owner_map):
    struct = jax.ShapeDtypeStruct
    place = jnp.stack([lax.axis_index("row"), lax.axis_index("col")]).astype(jnp.int32)
    weights = socs / jnp.sum(socs)
    owner = owner_map.reshape(1, DEV)

    def spread(taps, reverse):
        flat = taps.reshape(2 * CHAN, 2 * HALF + 1).astype(F32)
        gap = jnp.zeros((2 * CHAN, 2 * BLK - 2 * HALF - 1), F32)
        if reverse:
            return jnp.concatenate([flat[:, :1], gap, flat[:, :0:-1]], 1)
        return jnp.concatenate([flat, gap], 1)

    first = call(
        pack_kernel,
        struct((DEV * 8, BLK), BF),
        [HBM, HBM],
        [
            pltpu.SMEM((2, 3), jnp.int32),
            pltpu.VMEM((BLK, BLK), F32),
            pltpu.VMEM((COLS * 8, BLK), F32),
            pltpu.VMEM((COLS * 8, BLK), BF),
            pltpu.SemaphoreType.DMA,
            pltpu.SemaphoreType.DMA,
            pltpu.SemaphoreType.DMA((ROWS,)),
        ],
        "pack",
        out_space=HBM,
    )(in_hbm(cell_of_block), in_hbm(cells.reshape(BLK, BLK)))
    first = exchange(first.reshape(DEV, 8, BLK)).reshape(DEV * 8, BLK)

    picked, held, slots, by_owner = call(
        pick_kernel,
        (struct((COLS * PER_COL, BLK), BF), struct((BLK, BLK), F32), struct((DEV, BLK), F32), struct((DEV, DEV), BF)),
        [SMEM, VMEM, HBM],
        [
            pltpu.VMEM((1, DEV), jnp.int32),
            pltpu.VMEM((DEV * 8, BLK), F32),
            pltpu.VMEM((COLS, BLK), F32),
            pltpu.VMEM((COLS * PER_COL, BLK), F32),
            pltpu.SemaphoreType.DMA,
        ],
        "pick",
    )(place, first, in_hbm(owner))
    received = exchange(picked.reshape(COLS, PER_COL, BLK), "col").reshape(COLS * PER_COL, BLK)

    pieces = call(
        litho_kernel,
        struct((DEV * SLOTS, BLK), BF),
        [SMEM] + [VMEM] * 6,
        [
            pltpu.VMEM((DEV * SLOTS, BLK), F32),
            pltpu.VMEM((4, 384, BLK), F32),
            pltpu.VMEM((EXT_R, 512), BF),
            pltpu.VMEM((2, 384, TILE_C), BF),
            pltpu.VMEM((2, 384, TILE_C), BF),
            pltpu.VMEM((CHAN, TILE_R, TILE_C), F32),
            pltpu.VMEM((TILE_R, TILE_C), F32),
            pltpu.VMEM((384, 512), F32),
            pltpu.VMEM((EXT_R, 12 * BLK), BF),
            pltpu.VMEM((EXT_R, 12 * BLK), BF),
        ],
        "litho",
        32,
    )(
        weights, received, target,
        spread(row_taps, False), spread(row_taps, True),
        spread(col_taps, False), spread(col_taps, True),
    )
    pieces = exchange(pieces.reshape(DEV, SLOTS, BLK)).reshape(DEV * SLOTS, BLK)

    results = call(
        update_kernel,
        struct((DEV * 8, BLK), BF),
        [VMEM] * 4,
        [pltpu.VMEM((DEV * SLOTS, BLK), F32), pltpu.VMEM((DEV * 8, BLK), F32)],
        "update",
    )(pieces, slots, by_owner, held)
    results = exchange(results.reshape(DEV, 8, BLK)).reshape(DEV * 8, BLK)

    gradient, new_mask = call(
        unpack_kernel,
        (struct((BLK, BLK), F32), struct((TILE_R, TILE_C), F32)),
        [VMEM],
        [pltpu.VMEM((DEV * 8, BLK), F32), pltpu.VMEM((3, TILE_R, BLK), F32)],
        "unpack",
    )(results)
    return gradient.reshape(1, BLK, BLK), new_mask


def solution(mesh):
    in_specs = (P(AXES, None, None), P("row", "col"), P(), P(), P(), P("row", "col"), P())
    out_specs = (P(AXES, None, None), P("row", "col"))
    return jax.shard_map(
        per_device, mesh=mesh, in_specs=in_specs, out_specs=out_specs, check_vma=False
    )
```

```python
import jax
import jax.numpy as jnp
from jax import lax
from jax.experimental import pallas as pl
from jax.experimental.pallas import tpu as pltpu
from jax.sharding import PartitionSpec as P


AXES = ("row", "col")
ROWS, COLS = 4, 32
DEV = ROWS * COLS
BLK = 128
HALF = 17
TILE_R, TILE_C = 256, 384
COL_R = TILE_R + 72
FIELD_R = 304
SPLIT = 144
CHAN = 24
SLOTS = 8
PER_COL = 12 * ROWS
BF, F32 = jnp.bfloat16, jnp.float32


def dot(a, b):
    return lax.dot_general(a, b, (((1,), (0,)), ((), ())), preferred_element_type=F32)


def iota(dim, shape=(DEV, BLK)):
    return lax.broadcasted_iota(jnp.int32, shape, dim)


def slot_ids(ids, holder_col):
    lane, dev = iota(1), iota(0)
    dev_row, dev_col = dev // COLS, dev % COLS
    upper = ids
    lower = pltpu.roll(ids, BLK - 3, 1)
    above = jnp.where(dev_row == 0, -1.0, pltpu.roll(lower, COLS, 0))
    below = jnp.where(dev_row == ROWS - 1, -1.0, pltpu.roll(upper, DEV - COLS, 0))
    third = jnp.where(holder_col >= COLS // 2, above, below)
    out = jnp.full((DEV, BLK), -1.0, F32)
    for p, part in enumerate((upper, lower, third)):
        left = jnp.where(dev_col == 0, -1.0, pltpu.roll(part, 1, 0))
        right = jnp.where(dev_col == COLS - 1, -1.0, pltpu.roll(part, DEV - 1, 0))
        here = pltpu.roll(part, 4 * p, 1) if p else part
        out = jnp.where((lane >= 4 * p) & (lane < 4 * p + 3), here, out)
        out = jnp.where(lane == 4 * p + 3, pltpu.roll(left, 4 * p + 1, 1), out)
        out = jnp.where(lane == 12 + p, pltpu.roll(right, 12 + p, 1), out)
    return out


def owner_select(owner_ref, transpose):
    owner = jnp.broadcast_to(owner_ref[...], (DEV, DEV))
    if transpose:
        return (owner == iota(0)).astype(BF)
    return (owner.astype(F32).T == iota(1).astype(F32)).astype(BF)


def columns_of(slots, s):
    return jnp.broadcast_to(slots[:, s : s + 1], (slots.shape[0], BLK))


def pack_kernel(blocks_hbm, cells_hbm, out_hbm, blocks_ref, cells, stage, packed, ids_sem, in_sem, out_sem):
    fetch_ids = pltpu.make_async_copy(blocks_hbm, blocks_ref, ids_sem)
    fetch_ids.start()
    fetch = pltpu.make_async_copy(cells_hbm, cells, in_sem)
    fetch.start()
    lane = iota(1, (COLS, BLK))
    ids = jnp.full((COLS, BLK), -1.0, F32)
    for s in range(ROWS + 1, 8):
        stage[pl.ds(s, COLS, stride=8), :] = jnp.zeros((COLS, BLK), F32)
    fetch_ids.wait()
    for n in range(6):
        ids = jnp.where(lane == n, blocks_ref[n // 3, n % 3].astype(F32), ids)
    stage[pl.ds(ROWS, COLS, stride=8), :] = ids
    fetch.wait()
    for s in range(ROWS):
        stage[pl.ds(s, COLS, stride=8), :] = cells[pl.ds(s, COLS, stride=ROWS), :]
    packed[...] = stage[...].astype(BF)
    copies = [
        pltpu.make_async_copy(packed, out_hbm.at[pl.ds(r * COLS * 8, COLS * 8)], out_sem.at[r])
        for r in range(ROWS)
    ]
    for copy in copies:
        copy.start()
    for copy in copies:
        copy.wait()


def pick_kernel(
    place_ref, first_ref, owner_hbm, out_ref, held_ref, slots_ref, by_owner_ref,
    owner_ref, stage, mine, out_stage, sem,
):
    fetch = pltpu.make_async_copy(owner_hbm, owner_ref, sem)
    fetch.start()
    stage[...] = first_ref[...].astype(F32)
    slots = slot_ids(stage[pl.ds(ROWS, DEV, stride=8), :], place_ref[1])
    slots_ref[...] = slots
    table = jnp.concatenate([stage[pl.ds(s, DEV, stride=8), :] for s in range(ROWS)], 1)
    fetch.wait()
    by_owner_ref[...] = owner_select(owner_ref, True)
    held = dot(owner_select(owner_ref, False), table.astype(BF)).astype(BF)
    row = place_ref[0]
    own = held[:, :BLK].astype(F32)
    for s in range(1, ROWS):
        own = jnp.where(row == s, held[:, s * BLK : (s + 1) * BLK].astype(F32), own)
    held_ref[...] = own
    mine[...] = slots_ref[pl.ds(pl.multiple_of(row * COLS, COLS), COLS), :]
    here = mine[...]
    cell = iota(1, (COLS, BLK)).astype(F32)
    select = jnp.concatenate([(columns_of(here, s) == cell).astype(BF) for s in range(15)], 0)
    picked = dot(select, held)
    wide_lane = iota(1, (COLS, ROWS * BLK)) % BLK
    for t in range(12):
        made = picked[t * COLS : (t + 1) * COLS]
        if t % 4 == 3:
            at = (12 + t // 4) * COLS
            made = jnp.where(wide_lane >= BLK // 2, made, picked[at : at + COLS])
        for s in range(ROWS):
            out_stage[pl.ds(ROWS * t + s, COLS, stride=PER_COL), :] = made[:, s * BLK : (s + 1) * BLK]
    out_ref[...] = out_stage[...].astype(BF)


def toeplitz(taps_ref, m, rows=BLK):
    base = jnp.broadcast_to(taps_ref[pl.ds(m, 1), :], (rows, 2 * BLK))
    return pltpu.roll(base, 0, 1, stride=1, stride_axis=0).astype(BF)


def litho_kernel(
    place_ref, weights_ref, recv_ref, target_ref, row_ref, row_flip_ref, col_ref, col_rev_ref,
    out_ref, stage, wide, mask, columns_a, columns_b, field, light, grad, back_a, back_b,
):
    stage[...] = recv_ref[...].astype(F32)
    for q in range(4):
        for p in range(3):
            for s in range(ROWS):
                wide[q, pl.ds(p * BLK + s, COLS, stride=ROWS), :] = stage[
                    pl.ds(ROWS * (4 * p + q) + s, COLS, stride=PER_COL), :
                ]
    whole = jnp.concatenate([wide[q] for q in range(4)], 1)
    mask[...] = pltpu.roll(pltpu.roll(whole, HALF, 1), 2 * HALF, 0)[:COL_R].astype(BF)
    for columns in (columns_a, columns_b):
        columns[:, COL_R:, :] = jnp.zeros((2, SPLIT + 2 * BLK - COL_R, TILE_C), BF)
    light[...] = jnp.zeros_like(light)

    def make_columns(k, columns):
        rolled = [toeplitz(col_rev_ref, 2 * k + r) for r in range(2)]
        col_matrix = jnp.concatenate(
            [
                jnp.concatenate([t[:, :BLK] for t in rolled], 1),
                jnp.concatenate([t[:, BLK:] for t in rolled], 1),
            ],
            0,
        )
        for q in range(3):
            made = dot(mask[:, q * BLK : (q + 2) * BLK], col_matrix).astype(BF)
            for r in range(2):
                columns[r, :COL_R, q * BLK : (q + 1) * BLK] = made[:, r * BLK : (r + 1) * BLK]

    def make_field(k, columns):
        row_matrix = jnp.concatenate([toeplitz(row_ref, 2 * k + r, FIELD_R - SPLIT) for r in range(2)], 1)
        weight = weights_ref[k // 2]
        windows = [
            jnp.concatenate([columns[r, p * SPLIT : p * SPLIT + 2 * BLK, :] for r in range(2)], 0)
            for p in range(2)
        ]
        last = dot(row_matrix, jnp.concatenate([w[:, 2 * BLK :] for w in windows], 1))
        for p in range(2):
            made = jnp.concatenate(
                [dot(row_matrix, windows[p][:, : 2 * BLK]), last[:, p * BLK : (p + 1) * BLK]], 1
            )
            here = slice(p * SPLIT, FIELD_R if p else SPLIT)
            made = made[: here.stop - here.start]
            light[here] += weight * made * made
            field[k, here] = made

    make_columns(0, columns_a)

    buffers = (columns_a, columns_b)
    for k in range(CHAN):
        if k + 1 < CHAN:
            make_columns(k + 1, buffers[(k + 1) % 2])
        make_field(k, buffers[k % 2])
    resist = jax.nn.sigmoid(3.0 * (light[...] - 1.3))
    error = 2.0 * (resist - target_ref[...]) * 3.0 * resist * (1.0 - resist)
    at_row = iota(0, (FIELD_R, TILE_C))
    first = jnp.where(place_ref[0] == 0, HALF, 0)
    end = jnp.where(place_ref[0] == ROWS - 1, HALF + TILE_R, FIELD_R)
    light[...] = jnp.where((at_row >= first) & (at_row < end), error, 0.0)
    grad[...] = jnp.zeros_like(grad)

    def make_back(k, j, back):
        weighted = (2.0 * weights_ref[k // 2] * field[k] * light[...]).astype(BF)
        taps = jnp.concatenate([toeplitz(row_flip_ref, 2 * k + r) for r in range(2)], 0)
        windows = [
            weighted[: 2 * BLK],
            jnp.concatenate([weighted[BLK:], jnp.zeros((3 * BLK - FIELD_R, TILE_C), BF)], 0),
        ]
        last = dot(taps, jnp.concatenate([w[:, 2 * BLK :] for w in windows], 1)).astype(BF)
        parts = [dot(taps, w[:, : 2 * BLK]).astype(BF) for w in windows]
        for r in range(2):
            for q in range(3):
                at = (4 * q + 2 * j + r) * BLK
                for p in range(2):
                    piece = last if q == 2 else parts[p]
                    lanes = p * BLK if q == 2 else q * BLK
                    back[p * BLK : (p + 1) * BLK, at : at + BLK] = piece[
                        r * BLK : (r + 1) * BLK, lanes : lanes + BLK
                    ]

    def add_grad(k, back):
        col_matrix = jnp.concatenate([toeplitz(col_ref, 2 * k + r) for r in range(4)], 0)
        for q in range(3):
            grad[:, q * BLK : (q + 2) * BLK] += dot(
                back[:, 4 * q * BLK : 4 * (q + 1) * BLK], col_matrix
            )

    backs = (back_a, back_b)
    for j in range(2):
        make_back(j, j, back_a)
    for n in range(CHAN // 2):
        if n + 1 < CHAN // 2:
            for j in range(2):
                make_back(2 * n + 2 + j, j, backs[(n + 1) % 2])
        add_grad(2 * n, backs[n % 2])
    whole = pltpu.roll(grad[...], 512 - HALF, 1)
    for q in range(4):
        wide[q, :TILE_R] = whole[:, q * BLK : (q + 1) * BLK]
    for q in range(4):
        for p in range(2):
            for r in range(ROWS):
                stage[pl.ds(r * COLS * SLOTS + 4 * p + q, COLS, stride=SLOTS), :] = wide[
                    q, pl.ds(p * BLK + r, COLS, stride=ROWS), :
                ]
    out_ref[...] = stage[: DEV * SLOTS].astype(BF)


def update_kernel(recv_ref, slots_ref, by_owner_ref, held_ref, out_ref, stage, out_stage):
    lane = iota(1)
    slots = slots_ref[...]
    slots_t = slots.T
    cell_down = iota(0).astype(F32)
    stage[...] = recv_ref[...].astype(F32)

    def gather(s, piece):
        select = (jnp.broadcast_to(slots_t[s : s + 1, :], (BLK, DEV)) == cell_down).astype(BF)
        return dot(select, stage[pl.ds(piece, DEV, stride=SLOTS), :].astype(BF))

    total = jnp.zeros((BLK, BLK), F32)
    from_left, from_right = total, total
    for p in range(2):
        for q in range(3):
            total += gather(4 * p + q, 4 * p + q)
        from_left += gather(4 * p + 3, 4 * p + 3)
        from_right += gather(12 + p, 4 * p + 3)
    total += jnp.where(lane >= BLK // 2, from_left, from_right)
    updated = (held_ref[...] - 0.05 * total).astype(BF)
    cell = lane.astype(F32)
    for p in range(2):
        for q in range(3):
            select = (columns_of(slots, 4 * p + q) == cell).astype(BF)
            out_stage[pl.ds(3 * p + q, DEV, stride=8), :] = dot(select, updated)
    out_stage[pl.ds(6, DEV, stride=8), :] = dot(by_owner_ref[...], total.astype(BF))
    out_stage[pl.ds(7, DEV, stride=8), :] = jnp.zeros((DEV, BLK), F32)
    out_ref[...] = out_stage[...].astype(BF)


def unpack_kernel(recv_ref, grad_ref, mask_ref, stage, wide):
    stage[...] = recv_ref[...].astype(F32)
    for r in range(ROWS):
        for p in range(2):
            for q in range(3):
                wide[q, pl.ds(p * BLK + r, COLS, stride=ROWS), :] = stage[
                    pl.ds(r * COLS * 8 + 3 * p + q, COLS, stride=8), :
                ]
        grad_ref[pl.ds(r, COLS, stride=ROWS), :] = stage[pl.ds(r * COLS * 8 + 6, COLS, stride=8), :]
    for q in range(3):
        mask_ref[:, q * BLK : (q + 1) * BLK] = wide[q]


SMEM = pl.BlockSpec(memory_space=pltpu.SMEM)
VMEM = pl.BlockSpec(memory_space=pltpu.VMEM)
HBM = pl.BlockSpec(memory_space=pltpu.HBM)


def call(kernel, out_shape, in_specs, scratch, limit=8, out_space=VMEM):
    return pl.pallas_call(
        kernel,
        out_shape=out_shape,
        in_specs=in_specs,
        out_specs=jax.tree.map(lambda _: out_space, out_shape),
        scratch_shapes=scratch,
        compiler_params=pltpu.CompilerParams(vmem_limit_bytes=limit << 20),
    )


def in_hbm(x):
    return pltpu.with_memory_space_constraint(x, pltpu.HBM)


def exchange(x, axes=AXES):
    return lax.all_to_all(x, axes, 0, 0, tiled=True)


def per_device(cells, target, row_taps, col_taps, socs, cell_of_block, owner_map):
    struct = jax.ShapeDtypeStruct
    place = jnp.stack([lax.axis_index("row"), lax.axis_index("col")]).astype(jnp.int32)
    weights = socs / jnp.sum(socs)
    owner = owner_map.reshape(1, DEV)

    def spread(taps, reverse):
        flat = taps.reshape(2 * CHAN, 2 * HALF + 1).astype(F32)
        gap = jnp.zeros((2 * CHAN, 2 * BLK - 2 * HALF - 1), F32)
        if reverse:
            return jnp.concatenate([flat[:, :1], gap, flat[:, :0:-1]], 1)
        return jnp.concatenate([flat, gap], 1)

    down = [(i, i + 1) for i in range(ROWS - 1)]
    up = [(i + 1, i) for i in range(ROWS - 1)]
    above = lax.ppermute(target[TILE_R - HALF :], "row", down)
    below = lax.ppermute(target[:HALF], "row", up)
    wide_target = jnp.concatenate(
        [
            above,
            target,
            below,
            jnp.zeros((FIELD_R - TILE_R - 2 * HALF, TILE_C), F32),
        ],
        0,
    )

    first = call(
        pack_kernel,
        struct((DEV * 8, BLK), BF),
        [HBM, HBM],
        [
            pltpu.SMEM((2, 3), jnp.int32),
            pltpu.VMEM((BLK, BLK), F32),
            pltpu.VMEM((COLS * 8, BLK), F32),
            pltpu.VMEM((COLS * 8, BLK), BF),
            pltpu.SemaphoreType.DMA,
            pltpu.SemaphoreType.DMA,
            pltpu.SemaphoreType.DMA((ROWS,)),
        ],
        out_space=HBM,
    )(in_hbm(cell_of_block), in_hbm(cells.reshape(BLK, BLK)))
    first = exchange(first.reshape(DEV, 8, BLK))
    first = first.reshape(DEV * 8, BLK)

    picked, held, slots, by_owner = call(
        pick_kernel,
        (struct((COLS * PER_COL, BLK), BF), struct((BLK, BLK), F32), struct((DEV, BLK), F32), struct((DEV, DEV), BF)),
        [SMEM, VMEM, HBM],
        [
            pltpu.VMEM((1, DEV), jnp.int32),
            pltpu.VMEM((DEV * 8, BLK), F32),
            pltpu.VMEM((COLS, BLK), F32),
            pltpu.VMEM((COLS * PER_COL, BLK), F32),
            pltpu.SemaphoreType.DMA,
        ],
    )(place, first, in_hbm(owner))
    received = exchange(picked.reshape(COLS, PER_COL, BLK), "col")
    received = received.reshape(COLS * PER_COL, BLK)

    pieces = call(
        litho_kernel,
        struct((DEV * SLOTS, BLK), BF),
        [SMEM] * 2 + [VMEM] * 6,
        [
            pltpu.VMEM((COLS * PER_COL, BLK), F32),
            pltpu.VMEM((4, 384, BLK), F32),
            pltpu.VMEM((COL_R, 512), BF),
            pltpu.VMEM((2, SPLIT + 2 * BLK, TILE_C), BF),
            pltpu.VMEM((2, SPLIT + 2 * BLK, TILE_C), BF),
            pltpu.VMEM((CHAN, FIELD_R, TILE_C), F32),
            pltpu.VMEM((FIELD_R, TILE_C), F32),
            pltpu.VMEM((TILE_R, 512), F32),
            pltpu.VMEM((TILE_R, 12 * BLK), BF),
            pltpu.VMEM((TILE_R, 12 * BLK), BF),
        ],
        32,
    )(
        place, weights, received, wide_target,
        spread(row_taps, False), spread(row_taps[:, :, ::-1], False),
        spread(col_taps, False), spread(col_taps, True),
    )
    pieces = exchange(pieces.reshape(DEV, SLOTS, BLK)).reshape(DEV * SLOTS, BLK)

    results = call(
        update_kernel,
        struct((DEV * 8, BLK), BF),
        [VMEM] * 4,
        [pltpu.VMEM((DEV * SLOTS, BLK), F32), pltpu.VMEM((DEV * 8, BLK), F32)],
    )(pieces, slots, by_owner, held)
    results = exchange(results.reshape(DEV, 8, BLK)).reshape(DEV * 8, BLK)

    gradient, new_mask = call(
        unpack_kernel,
        (struct((BLK, BLK), F32), struct((TILE_R, TILE_C), F32)),
        [VMEM],
        [pltpu.VMEM((DEV * 8, BLK), F32), pltpu.VMEM((3, TILE_R, BLK), F32)],
    )(results)
    return gradient.reshape(1, BLK, BLK), new_mask


def solution(mesh):
    in_specs = (P(AXES, None, None), P("row", "col"), P(), P(), P(), P("row", "col"), P())
    out_specs = (P(AXES, None, None), P("row", "col"))
    return jax.shard_map(
        per_device, mesh=mesh, in_specs=in_specs, out_specs=out_specs, check_vma=False
    )
```

```python
import jax
import jax.numpy as jnp
from jax import lax
from jax.experimental import pallas as pl
from jax.experimental.pallas import tpu as pltpu
from jax.sharding import PartitionSpec as P


AXES = ("row", "col")
ROWS, COLS = 4, 32
DEV = ROWS * COLS
BLK = 128
HALF = 17
TILE_R, TILE_C = 256, 384
COL_R = TILE_R + 72
FIELD_R = 304
STEP = 80
STEPS = 4
COL_ROWS = (STEPS - 1) * STEP + BLK
CHAN = 24
SLOTS = 8
PER_COL = 12 * ROWS
BF, F32 = jnp.bfloat16, jnp.float32


def dot(a, b):
    return lax.dot_general(a, b, (((1,), (0,)), ((), ())), preferred_element_type=F32)


def iota(dim, shape=(DEV, BLK)):
    return lax.broadcasted_iota(jnp.int32, shape, dim)


def slot_ids(ids, holder_col):
    lane, dev = iota(1), iota(0)
    dev_row, dev_col = dev // COLS, dev % COLS
    upper = ids
    lower = pltpu.roll(ids, BLK - 3, 1)
    above = jnp.where(dev_row == 0, -1.0, pltpu.roll(lower, COLS, 0))
    below = jnp.where(dev_row == ROWS - 1, -1.0, pltpu.roll(upper, DEV - COLS, 0))
    third = jnp.where(holder_col >= COLS // 2, above, below)
    out = jnp.full((DEV, BLK), -1.0, F32)
    for p, part in enumerate((upper, lower, third)):
        left = jnp.where(dev_col == 0, -1.0, pltpu.roll(part, 1, 0))
        right = jnp.where(dev_col == COLS - 1, -1.0, pltpu.roll(part, DEV - 1, 0))
        here = pltpu.roll(part, 4 * p, 1) if p else part
        out = jnp.where((lane >= 4 * p) & (lane < 4 * p + 3), here, out)
        out = jnp.where(lane == 4 * p + 3, pltpu.roll(left, 4 * p + 1, 1), out)
        out = jnp.where(lane == 12 + p, pltpu.roll(right, 12 + p, 1), out)
    return out


def owner_select(owner_ref, transpose):
    owner = jnp.broadcast_to(owner_ref[...], (DEV, DEV))
    if transpose:
        return (owner == iota(0)).astype(BF)
    return (owner.astype(F32).T == iota(1).astype(F32)).astype(BF)


def columns_of(slots, s):
    return jnp.broadcast_to(slots[:, s : s + 1], (slots.shape[0], BLK))


def pack_kernel(
    blocks_hbm, cells_hbm, owner_hbm, out_hbm, by_cell_ref, by_owner_ref,
    blocks_ref, owner_ref, cells, stage, packed, ids_sem, owner_sem, in_sem, out_sem,
):
    fetch_ids = pltpu.make_async_copy(blocks_hbm, blocks_ref, ids_sem)
    fetch_ids.start()
    fetch = pltpu.make_async_copy(cells_hbm, cells, in_sem)
    fetch.start()
    fetch_owner = pltpu.make_async_copy(owner_hbm, owner_ref, owner_sem)
    fetch_owner.start()
    lane = iota(1, (COLS, BLK))
    ids = jnp.full((COLS, BLK), -1.0, F32)
    for s in range(ROWS + 1, 8):
        stage[pl.ds(s, COLS, stride=8), :] = jnp.zeros((COLS, BLK), F32)
    fetch_ids.wait()
    for n in range(6):
        ids = jnp.where(lane == n, blocks_ref[n // 3, n % 3].astype(F32), ids)
    stage[pl.ds(ROWS, COLS, stride=8), :] = ids
    fetch.wait()
    for s in range(ROWS):
        stage[pl.ds(s, COLS, stride=8), :] = cells[pl.ds(s, COLS, stride=ROWS), :]
    packed[...] = stage[...].astype(BF)
    copies = [
        pltpu.make_async_copy(packed, out_hbm.at[pl.ds(r * COLS * 8, COLS * 8)], out_sem.at[r])
        for r in range(ROWS)
    ]
    for copy in copies:
        copy.start()
    fetch_owner.wait()
    by_cell_ref[...] = owner_select(owner_ref, False)
    by_owner_ref[...] = owner_select(owner_ref, True)
    for copy in copies:
        copy.wait()


def pick_kernel(
    place_ref, first_ref, by_cell_ref, out_ref, held_ref, slots_ref, stage, mine, out_stage,
):
    stage[...] = first_ref[...].astype(F32)
    slots = slot_ids(stage[pl.ds(ROWS, DEV, stride=8), :], place_ref[1])
    slots_ref[...] = slots
    table = jnp.concatenate([stage[pl.ds(s, DEV, stride=8), :] for s in range(ROWS)], 1)
    held = dot(by_cell_ref[...], table.astype(BF)).astype(BF)
    row = place_ref[0]
    own = held[:, :BLK].astype(F32)
    for s in range(1, ROWS):
        own = jnp.where(row == s, held[:, s * BLK : (s + 1) * BLK].astype(F32), own)
    held_ref[...] = own
    mine[...] = slots_ref[pl.ds(pl.multiple_of(row * COLS, COLS), COLS), :]
    here = mine[...]
    cell = iota(1, (COLS, BLK)).astype(F32)
    select = jnp.concatenate([(columns_of(here, s) == cell).astype(BF) for s in range(15)], 0)
    picked = dot(select, held)
    wide_lane = iota(1, (COLS, ROWS * BLK)) % BLK
    for t in range(12):
        made = picked[t * COLS : (t + 1) * COLS]
        if t % 4 == 3:
            at = (12 + t // 4) * COLS
            made = jnp.where(wide_lane >= BLK // 2, made, picked[at : at + COLS])
        for s in range(ROWS):
            out_stage[pl.ds(ROWS * t + s, COLS, stride=PER_COL), :] = made[:, s * BLK : (s + 1) * BLK]
    out_ref[...] = out_stage[...].astype(BF)


def toeplitz(taps_ref, m, rows=BLK, lanes=2 * BLK):
    base = jnp.broadcast_to(taps_ref[pl.ds(m, 1), :lanes], (rows, lanes))
    return pltpu.roll(base, 0, 1, stride=1, stride_axis=0).astype(BF)


def litho_kernel(
    place_ref, socs_ref, recv_ref, target_ref, row_ref, row_flip_ref, col_ref, col_rev_ref,
    out_ref, stage, wide, mask, columns_a, columns_b, field, light, grad, back_a, back_b,
):
    stage[...] = recv_ref[...].astype(F32)
    for q in range(4):
        for p in range(3):
            for s in range(ROWS):
                wide[q, pl.ds(p * BLK + s, COLS, stride=ROWS), :] = stage[
                    pl.ds(ROWS * (4 * p + q) + s, COLS, stride=PER_COL), :
                ]
    whole = jnp.concatenate([wide[q] for q in range(4)], 1)
    mask[...] = pltpu.roll(pltpu.roll(whole, HALF, 1), 2 * HALF, 0)[:COL_R].astype(BF)
    for columns in (columns_a, columns_b):
        columns[:, COL_R:, :] = jnp.zeros((2, COL_ROWS - COL_R, TILE_C), BF)
    light[...] = jnp.zeros_like(light)

    def make_columns(k, columns):
        rolled = [toeplitz(col_rev_ref, 2 * k + r) for r in range(2)]
        col_matrix = jnp.concatenate(
            [
                jnp.concatenate([t[:, :BLK] for t in rolled], 1),
                jnp.concatenate([t[:, BLK:] for t in rolled], 1),
            ],
            0,
        )
        for q in range(3):
            made = dot(mask[:, q * BLK : (q + 2) * BLK], col_matrix).astype(BF)
            for r in range(2):
                columns[r, :COL_R, q * BLK : (q + 1) * BLK] = made[:, r * BLK : (r + 1) * BLK]

    def make_field(k, columns):
        row_matrix = jnp.concatenate([toeplitz(row_ref, 2 * k + r, STEP, BLK) for r in range(2)], 1)
        weight = socs_ref[k // 2]
        windows = [
            jnp.concatenate([columns[r, p * STEP : p * STEP + BLK, :] for r in range(2)], 0)
            for p in range(STEPS)
        ]
        for p in range(STEPS):
            if p % 2 == 0:
                pair = jnp.concatenate([w[:, 2 * BLK :] for w in windows[p : p + 2]], 1)
                last = dot(row_matrix, pair)
            at = p % 2 * BLK
            made = jnp.concatenate(
                [dot(row_matrix, windows[p][:, : 2 * BLK]), last[:, at : at + BLK]], 1
            )
            here = slice(p * STEP, min((p + 1) * STEP, FIELD_R))
            made = made[: here.stop - here.start]
            light[here] += weight * made * made
            field[k, here] = made

    make_columns(0, columns_a)

    buffers = (columns_a, columns_b)
    for k in range(CHAN):
        if k + 1 < CHAN:
            make_columns(k + 1, buffers[(k + 1) % 2])
        make_field(k, buffers[k % 2])
    total = socs_ref[0]
    for n in range(1, CHAN // 2):
        total += socs_ref[n]
    total = jnp.full((1, TILE_C), total, F32)
    resist = jax.nn.sigmoid(3.0 * (light[...] / total - 1.3))
    error = 2.0 * (resist - target_ref[...]) * 3.0 * resist * (1.0 - resist)
    at_row = iota(0, (FIELD_R, TILE_C))
    first = jnp.where(place_ref[0] == 0, HALF, 0)
    end = jnp.where(place_ref[0] == ROWS - 1, HALF + TILE_R, FIELD_R)
    light[...] = jnp.where((at_row >= first) & (at_row < end), error * (2.0 / total), 0.0)
    grad[...] = jnp.zeros_like(grad)

    def make_back(k, j, back):
        weighted = (socs_ref[k // 2] * field[k] * light[...]).astype(BF)
        taps = jnp.concatenate([toeplitz(row_flip_ref, 2 * k + r) for r in range(2)], 0)
        windows = [
            weighted[: 2 * BLK],
            jnp.concatenate([weighted[BLK:], jnp.zeros((3 * BLK - FIELD_R, TILE_C), BF)], 0),
        ]
        last = dot(taps, jnp.concatenate([w[:, 2 * BLK :] for w in windows], 1)).astype(BF)
        parts = [dot(taps, w[:, : 2 * BLK]).astype(BF) for w in windows]
        for r in range(2):
            for q in range(3):
                at = (4 * q + 2 * j + r) * BLK
                for p in range(2):
                    piece = last if q == 2 else parts[p]
                    lanes = p * BLK if q == 2 else q * BLK
                    back[p * BLK : (p + 1) * BLK, at : at + BLK] = piece[
                        r * BLK : (r + 1) * BLK, lanes : lanes + BLK
                    ]

    def add_grad(k, back):
        col_matrix = jnp.concatenate([toeplitz(col_ref, 2 * k + r) for r in range(4)], 0)
        for q in range(3):
            grad[:, q * BLK : (q + 2) * BLK] += dot(
                back[:, 4 * q * BLK : 4 * (q + 1) * BLK], col_matrix
            )

    backs = (back_a, back_b)
    for j in range(2):
        make_back(j, j, back_a)
    for n in range(CHAN // 2):
        if n + 1 < CHAN // 2:
            for j in range(2):
                make_back(2 * n + 2 + j, j, backs[(n + 1) % 2])
        add_grad(2 * n, backs[n % 2])
    whole = pltpu.roll(grad[...], 512 - HALF, 1)
    for q in range(4):
        wide[q, :TILE_R] = whole[:, q * BLK : (q + 1) * BLK]
    for q in range(4):
        for p in range(2):
            for r in range(ROWS):
                stage[pl.ds(r * COLS * SLOTS + 4 * p + q, COLS, stride=SLOTS), :] = wide[
                    q, pl.ds(p * BLK + r, COLS, stride=ROWS), :
                ]
    out_ref[...] = stage[: DEV * SLOTS].astype(BF)


def update_kernel(recv_ref, slots_ref, by_owner_ref, held_ref, out_ref, stage, out_stage):
    lane = iota(1)
    slots = slots_ref[...]
    slots_t = slots.T
    cell_down = iota(0).astype(F32)
    stage[...] = recv_ref[...].astype(F32)

    def gather(s, piece):
        select = (jnp.broadcast_to(slots_t[s : s + 1, :], (BLK, DEV)) == cell_down).astype(BF)
        return dot(select, stage[pl.ds(piece, DEV, stride=SLOTS), :].astype(BF))

    total = jnp.zeros((BLK, BLK), F32)
    from_left, from_right = total, total
    for p in range(2):
        for q in range(3):
            total += gather(4 * p + q, 4 * p + q)
        from_left += gather(4 * p + 3, 4 * p + 3)
        from_right += gather(12 + p, 4 * p + 3)
    total += jnp.where(lane >= BLK // 2, from_left, from_right)
    updated = (held_ref[...] - 0.05 * total).astype(BF)
    cell = lane.astype(F32)
    for p in range(2):
        for q in range(3):
            select = (columns_of(slots, 4 * p + q) == cell).astype(BF)
            out_stage[pl.ds(3 * p + q, DEV, stride=8), :] = dot(select, updated)
    out_stage[pl.ds(6, DEV, stride=8), :] = dot(by_owner_ref[...], total.astype(BF))
    out_stage[pl.ds(7, DEV, stride=8), :] = jnp.zeros((DEV, BLK), F32)
    out_ref[...] = out_stage[...].astype(BF)


def unpack_kernel(recv_ref, grad_ref, mask_ref, stage, wide):
    stage[...] = recv_ref[...].astype(F32)
    for r in range(ROWS):
        for p in range(2):
            for q in range(3):
                wide[q, pl.ds(p * BLK + r, COLS, stride=ROWS), :] = stage[
                    pl.ds(r * COLS * 8 + 3 * p + q, COLS, stride=8), :
                ]
        grad_ref[pl.ds(r, COLS, stride=ROWS), :] = stage[pl.ds(r * COLS * 8 + 6, COLS, stride=8), :]
    for q in range(3):
        mask_ref[:, q * BLK : (q + 1) * BLK] = wide[q]


SMEM = pl.BlockSpec(memory_space=pltpu.SMEM)
VMEM = pl.BlockSpec(memory_space=pltpu.VMEM)
HBM = pl.BlockSpec(memory_space=pltpu.HBM)


def call(kernel, out_shape, in_specs, scratch, limit=8, out_space=None):
    return pl.pallas_call(
        kernel,
        out_shape=out_shape,
        in_specs=in_specs,
        out_specs=out_space or jax.tree.map(lambda _: VMEM, out_shape),
        scratch_shapes=scratch,
        compiler_params=pltpu.CompilerParams(vmem_limit_bytes=limit << 20),
    )


def in_hbm(x):
    return pltpu.with_memory_space_constraint(x, pltpu.HBM)


def exchange(x, axes=AXES):
    return lax.all_to_all(x, axes, 0, 0, tiled=True)


def per_device(cells, target, row_taps, col_taps, socs, cell_of_block, owner_map):
    struct = jax.ShapeDtypeStruct
    place = jnp.stack([lax.axis_index("row"), lax.axis_index("col")]).astype(jnp.int32)
    owner = owner_map.reshape(1, DEV)

    def spread(taps, reverse):
        flat = taps.reshape(2 * CHAN, 2 * HALF + 1).astype(F32)
        gap = jnp.zeros((2 * CHAN, 2 * BLK - 2 * HALF - 1), F32)
        if reverse:
            return jnp.concatenate([flat[:, :1], gap, flat[:, :0:-1]], 1)
        return jnp.concatenate([flat, gap], 1)

    down = [(i, i + 1) for i in range(ROWS - 1)]
    up = [(i + 1, i) for i in range(ROWS - 1)]
    above = lax.ppermute(target[TILE_R - HALF :], "row", down)
    below = lax.ppermute(target[:HALF], "row", up)
    wide_target = jnp.concatenate(
        [
            above,
            target,
            below,
            jnp.zeros((FIELD_R - TILE_R - 2 * HALF, TILE_C), F32),
        ],
        0,
    )

    select = struct((DEV, DEV), BF)
    first, by_cell, by_owner = call(
        pack_kernel,
        (struct((DEV * 8, BLK), BF), select, select),
        [HBM, HBM, HBM],
        [
            pltpu.SMEM((2, 3), jnp.int32),
            pltpu.VMEM((1, DEV), jnp.int32),
            pltpu.VMEM((BLK, BLK), F32),
            pltpu.VMEM((COLS * 8, BLK), F32),
            pltpu.VMEM((COLS * 8, BLK), BF),
            pltpu.SemaphoreType.DMA,
            pltpu.SemaphoreType.DMA,
            pltpu.SemaphoreType.DMA,
            pltpu.SemaphoreType.DMA((ROWS,)),
        ],
        out_space=(HBM, VMEM, VMEM),
    )(in_hbm(cell_of_block), in_hbm(cells.reshape(BLK, BLK)), in_hbm(owner))
    first = exchange(first.reshape(DEV, 8, BLK))
    first = first.reshape(DEV * 8, BLK)

    picked, held, slots = call(
        pick_kernel,
        (struct((COLS * PER_COL, BLK), BF), struct((BLK, BLK), F32), struct((DEV, BLK), F32)),
        [SMEM, VMEM, VMEM],
        [
            pltpu.VMEM((DEV * 8, BLK), F32),
            pltpu.VMEM((COLS, BLK), F32),
            pltpu.VMEM((COLS * PER_COL, BLK), F32),
        ],
    )(place, first, by_cell)
    received = exchange(picked.reshape(COLS, PER_COL, BLK), "col")
    received = received.reshape(COLS * PER_COL, BLK)

    pieces = call(
        litho_kernel,
        struct((DEV * SLOTS, BLK), BF),
        [SMEM] * 2 + [VMEM] * 6,
        [
            pltpu.VMEM((COLS * PER_COL, BLK), F32),
            pltpu.VMEM((4, 384, BLK), F32),
            pltpu.VMEM((COL_R, 512), BF),
            pltpu.VMEM((2, COL_ROWS, TILE_C), BF),
            pltpu.VMEM((2, COL_ROWS, TILE_C), BF),
            pltpu.VMEM((CHAN, FIELD_R, TILE_C), F32),
            pltpu.VMEM((FIELD_R, TILE_C), F32),
            pltpu.VMEM((TILE_R, 512), F32),
            pltpu.VMEM((TILE_R, 12 * BLK), BF),
            pltpu.VMEM((TILE_R, 12 * BLK), BF),
        ],
        32,
    )(
        place, in_hbm(socs), received, wide_target,
        spread(row_taps, False), spread(row_taps[:, :, ::-1], False),
        spread(col_taps, False), spread(col_taps, True),
    )
    pieces = exchange(pieces.reshape(DEV, SLOTS, BLK)).reshape(DEV * SLOTS, BLK)

    results = call(
        update_kernel,
        struct((DEV * 8, BLK), BF),
        [VMEM] * 4,
        [pltpu.VMEM((DEV * SLOTS, BLK), F32), pltpu.VMEM((DEV * 8, BLK), F32)],
    )(pieces, slots, by_owner, held)
    results = exchange(results.reshape(DEV, 8, BLK)).reshape(DEV * 8, BLK)

    gradient, new_mask = call(
        unpack_kernel,
        (struct((BLK, BLK), F32), struct((TILE_R, TILE_C), F32)),
        [VMEM],
        [pltpu.VMEM((DEV * 8, BLK), F32), pltpu.VMEM((3, TILE_R, BLK), F32)],
    )(results)
    return gradient.reshape(1, BLK, BLK), new_mask


def solution(mesh):
    in_specs = (P(AXES, None, None), P("row", "col"), P(), P(), P(), P("row", "col"), P())
    out_specs = (P(AXES, None, None), P("row", "col"))
    return jax.shard_map(
        per_device, mesh=mesh, in_specs=in_specs, out_specs=out_specs, check_vma=False
    )
```

```python
import jax
import jax.numpy as jnp
from jax import lax
from jax.experimental import pallas as pl
from jax.experimental.pallas import tpu as pltpu
from jax.sharding import PartitionSpec as P


AXES = ("row", "col")
ROWS, COLS = 4, 32
DEV = ROWS * COLS
BLK = 128
HALF = 17
TILE_R, TILE_C = 256, 384
COL_R = TILE_R + 72
FIELD_R = 304
STEP = 80
STEPS = 4
COL_ROWS = (STEPS - 1) * STEP + BLK
CHAN = 24
SLOTS = 8
PER_COL = 12 * ROWS
BF, F32 = jnp.bfloat16, jnp.float32


def dot(a, b):
    return lax.dot_general(a, b, (((1,), (0,)), ((), ())), preferred_element_type=F32)


def iota(dim, shape=(DEV, BLK)):
    return lax.broadcasted_iota(jnp.int32, shape, dim)


def slot_ids(ids, holder_col):
    lane, dev = iota(1), iota(0)
    dev_row, dev_col = dev // COLS, dev % COLS
    upper = ids
    lower = pltpu.roll(ids, BLK - 3, 1)
    above = jnp.where(dev_row == 0, -1.0, pltpu.roll(lower, COLS, 0))
    below = jnp.where(dev_row == ROWS - 1, -1.0, pltpu.roll(upper, DEV - COLS, 0))
    third = jnp.where(holder_col >= COLS // 2, above, below)
    out = jnp.full((DEV, BLK), -1.0, F32)
    for p, part in enumerate((upper, lower, third)):
        left = jnp.where(dev_col == 0, -1.0, pltpu.roll(part, 1, 0))
        right = jnp.where(dev_col == COLS - 1, -1.0, pltpu.roll(part, DEV - 1, 0))
        here = pltpu.roll(part, 4 * p, 1) if p else part
        out = jnp.where((lane >= 4 * p) & (lane < 4 * p + 3), here, out)
        out = jnp.where(lane == 4 * p + 3, pltpu.roll(left, 4 * p + 1, 1), out)
        out = jnp.where(lane == 12 + p, pltpu.roll(right, 12 + p, 1), out)
    return out


def owner_select(owner_ref, transpose):
    owner = jnp.broadcast_to(owner_ref[...], (DEV, DEV))
    if transpose:
        return (owner == iota(0)).astype(BF)
    return (owner.astype(F32).T == iota(1).astype(F32)).astype(BF)


def columns_of(slots, s):
    return jnp.broadcast_to(slots[:, s : s + 1], (slots.shape[0], BLK))


def pack_kernel(
    blocks_hbm, cells_hbm, owner_hbm, out_hbm, by_cell_ref, by_owner_ref,
    blocks_ref, owner_ref, cells, stage, packed, ids_sem, owner_sem, in_sem, out_sem,
):
    fetch_ids = pltpu.make_async_copy(blocks_hbm, blocks_ref, ids_sem)
    fetch_ids.start()
    fetch = pltpu.make_async_copy(cells_hbm, cells, in_sem)
    fetch.start()
    fetch_owner = pltpu.make_async_copy(owner_hbm, owner_ref, owner_sem)
    fetch_owner.start()
    lane = iota(1, (COLS, BLK))
    ids = jnp.full((COLS, BLK), -1.0, F32)
    for s in range(ROWS + 1, 8):
        stage[pl.ds(s, COLS, stride=8), :] = jnp.zeros((COLS, BLK), F32)
    fetch_ids.wait()
    for n in range(6):
        ids = jnp.where(lane == n, blocks_ref[n // 3, n % 3].astype(F32), ids)
    stage[pl.ds(ROWS, COLS, stride=8), :] = ids
    fetch.wait()
    for s in range(ROWS):
        stage[pl.ds(s, COLS, stride=8), :] = cells[pl.ds(s, COLS, stride=ROWS), :]
    packed[...] = stage[...].astype(BF)
    copies = [
        pltpu.make_async_copy(packed, out_hbm.at[pl.ds(r * COLS * 8, COLS * 8)], out_sem.at[r])
        for r in range(ROWS)
    ]
    for copy in copies:
        copy.start()
    fetch_owner.wait()
    by_cell_ref[...] = owner_select(owner_ref, False)
    by_owner_ref[...] = owner_select(owner_ref, True)
    for copy in copies:
        copy.wait()


def pick_kernel(
    place_ref, first_ref, by_cell_ref, out_hbm, held_ref, slots_ref,
    stage, mine, out_stage, packed, sem,
):
    stage[...] = first_ref[...].astype(F32)
    slots = slot_ids(stage[pl.ds(ROWS, DEV, stride=8), :], place_ref[1])
    slots_ref[...] = slots
    table = jnp.concatenate([stage[pl.ds(s, DEV, stride=8), :] for s in range(ROWS)], 1)
    held = dot(by_cell_ref[...], table.astype(BF)).astype(BF)
    row = place_ref[0]
    own = held[:, :BLK].astype(F32)
    for s in range(1, ROWS):
        own = jnp.where(row == s, held[:, s * BLK : (s + 1) * BLK].astype(F32), own)
    held_ref[...] = own
    mine[...] = slots_ref[pl.ds(pl.multiple_of(row * COLS, COLS), COLS), :]
    here = mine[...]
    cell = iota(1, (COLS, BLK)).astype(F32)
    select = jnp.concatenate([(columns_of(here, s) == cell).astype(BF) for s in range(15)], 0)
    picked = dot(select, held)
    wide_lane = iota(1, (COLS, ROWS * BLK)) % BLK
    for t in range(12):
        made = picked[t * COLS : (t + 1) * COLS]
        if t % 4 == 3:
            at = (12 + t // 4) * COLS
            made = jnp.where(wide_lane >= BLK // 2, made, picked[at : at + COLS])
        for s in range(ROWS):
            out_stage[pl.ds(ROWS * t + s, COLS, stride=PER_COL), :] = made[:, s * BLK : (s + 1) * BLK]
    part = COLS * PER_COL // ROWS
    copies = []
    for n in range(ROWS):
        here = pl.ds(n * part, part)
        packed[here, :] = out_stage[here, :].astype(BF)
        copies.append(pltpu.make_async_copy(packed.at[here], out_hbm.at[here], sem.at[n]))
        copies[n].start()
    for copy in copies:
        copy.wait()


def toeplitz(taps_ref, m, rows=BLK, lanes=2 * BLK):
    base = jnp.broadcast_to(taps_ref[pl.ds(m, 1), :lanes], (rows, lanes))
    return pltpu.roll(base, 0, 1, stride=1, stride_axis=0).astype(BF)


def litho_kernel(
    place_ref, socs_ref, recv_ref, target_ref, row_ref, row_flip_ref, col_ref, col_rev_ref,
    out_ref, stage, wide, mask, columns_a, columns_b, field, light, grad, back_a, back_b,
):
    stage[...] = recv_ref[...].astype(F32)
    for q in range(4):
        for p in range(3):
            for s in range(ROWS):
                wide[q, pl.ds(p * BLK + s, COLS, stride=ROWS), :] = stage[
                    pl.ds(ROWS * (4 * p + q) + s, COLS, stride=PER_COL), :
                ]
    whole = jnp.concatenate([wide[q] for q in range(4)], 1)
    mask[...] = pltpu.roll(pltpu.roll(whole, HALF, 1), 2 * HALF, 0)[:COL_R].astype(BF)
    for columns in (columns_a, columns_b):
        columns[:, COL_R:, :] = jnp.zeros((2, COL_ROWS - COL_R, TILE_C), BF)
    light[...] = jnp.zeros_like(light)

    def make_columns(k, columns):
        rolled = [toeplitz(col_rev_ref, 2 * k + r) for r in range(2)]
        col_matrix = jnp.concatenate(
            [
                jnp.concatenate([t[:, :BLK] for t in rolled], 1),
                jnp.concatenate([t[:, BLK:] for t in rolled], 1),
            ],
            0,
        )
        for q in range(3):
            made = dot(mask[:, q * BLK : (q + 2) * BLK], col_matrix).astype(BF)
            for r in range(2):
                columns[r, :COL_R, q * BLK : (q + 1) * BLK] = made[:, r * BLK : (r + 1) * BLK]

    def make_field(k, columns):
        row_matrix = jnp.concatenate([toeplitz(row_ref, 2 * k + r, STEP, BLK) for r in range(2)], 1)
        weight = socs_ref[k // 2]
        windows = [
            jnp.concatenate([columns[r, p * STEP : p * STEP + BLK, :] for r in range(2)], 0)
            for p in range(STEPS)
        ]
        for p in range(STEPS):
            if p % 2 == 0:
                pair = jnp.concatenate([w[:, 2 * BLK :] for w in windows[p : p + 2]], 1)
                last = dot(row_matrix, pair)
            at = p % 2 * BLK
            made = jnp.concatenate(
                [dot(row_matrix, windows[p][:, : 2 * BLK]), last[:, at : at + BLK]], 1
            )
            here = slice(p * STEP, min((p + 1) * STEP, FIELD_R))
            made = made[: here.stop - here.start]
            light[here] += weight * made * made
            field[k, here] = made

    make_columns(0, columns_a)

    buffers = (columns_a, columns_b)
    for k in range(CHAN):
        if k + 1 < CHAN:
            make_columns(k + 1, buffers[(k + 1) % 2])
        make_field(k, buffers[k % 2])
    total = socs_ref[0]
    for n in range(1, CHAN // 2):
        total += socs_ref[n]
    total = jnp.full((1, TILE_C), total, F32)
    resist = jax.nn.sigmoid(3.0 * (light[...] / total - 1.3))
    error = 2.0 * (resist - target_ref[...]) * 3.0 * resist * (1.0 - resist)
    at_row = iota(0, (FIELD_R, TILE_C))
    first = jnp.where(place_ref[0] == 0, HALF, 0)
    end = jnp.where(place_ref[0] == ROWS - 1, HALF + TILE_R, FIELD_R)
    light[...] = jnp.where((at_row >= first) & (at_row < end), error * (2.0 / total), 0.0)
    grad[...] = jnp.zeros_like(grad)

    def make_back(k, j, back):
        weighted = (socs_ref[k // 2] * field[k] * light[...]).astype(BF)
        taps = jnp.concatenate([toeplitz(row_flip_ref, 2 * k + r) for r in range(2)], 0)
        windows = [
            weighted[: 2 * BLK],
            jnp.concatenate([weighted[BLK:], jnp.zeros((3 * BLK - FIELD_R, TILE_C), BF)], 0),
        ]
        last = dot(taps, jnp.concatenate([w[:, 2 * BLK :] for w in windows], 1)).astype(BF)
        parts = [dot(taps, w[:, : 2 * BLK]).astype(BF) for w in windows]
        for r in range(2):
            for q in range(3):
                at = (4 * q + 2 * j + r) * BLK
                for p in range(2):
                    piece = last if q == 2 else parts[p]
                    lanes = p * BLK if q == 2 else q * BLK
                    back[p * BLK : (p + 1) * BLK, at : at + BLK] = piece[
                        r * BLK : (r + 1) * BLK, lanes : lanes + BLK
                    ]

    def add_grad(k, back):
        col_matrix = jnp.concatenate([toeplitz(col_ref, 2 * k + r) for r in range(4)], 0)
        for q in range(3):
            grad[:, q * BLK : (q + 2) * BLK] += dot(
                back[:, 4 * q * BLK : 4 * (q + 1) * BLK], col_matrix
            )

    backs = (back_a, back_b)
    for j in range(2):
        make_back(j, j, back_a)
    for n in range(CHAN // 2):
        if n + 1 < CHAN // 2:
            for j in range(2):
                make_back(2 * n + 2 + j, j, backs[(n + 1) % 2])
        add_grad(2 * n, backs[n % 2])
    whole = pltpu.roll(grad[...], 512 - HALF, 1)
    for q in range(4):
        wide[q, :TILE_R] = whole[:, q * BLK : (q + 1) * BLK]
    for q in range(4):
        for p in range(2):
            for r in range(ROWS):
                stage[pl.ds(r * COLS * SLOTS + 4 * p + q, COLS, stride=SLOTS), :] = wide[
                    q, pl.ds(p * BLK + r, COLS, stride=ROWS), :
                ]
    out_ref[...] = stage[: DEV * SLOTS].astype(BF)


def update_kernel(recv_ref, slots_ref, by_owner_ref, held_ref, out_ref, stage, out_stage):
    lane = iota(1)
    slots = slots_ref[...]
    slots_t = slots.T
    cell_down = iota(0).astype(F32)
    stage[...] = recv_ref[...].astype(F32)

    def gather(s, piece):
        select = (jnp.broadcast_to(slots_t[s : s + 1, :], (BLK, DEV)) == cell_down).astype(BF)
        return dot(select, stage[pl.ds(piece, DEV, stride=SLOTS), :].astype(BF))

    total = jnp.zeros((BLK, BLK), F32)
    from_left, from_right = total, total
    for p in range(2):
        for q in range(3):
            total += gather(4 * p + q, 4 * p + q)
        from_left += gather(4 * p + 3, 4 * p + 3)
        from_right += gather(12 + p, 4 * p + 3)
    total += jnp.where(lane >= BLK // 2, from_left, from_right)
    updated = (held_ref[...] - 0.05 * total).astype(BF)
    cell = lane.astype(F32)
    for p in range(2):
        for q in range(3):
            select = (columns_of(slots, 4 * p + q) == cell).astype(BF)
            out_stage[pl.ds(3 * p + q, DEV, stride=8), :] = dot(select, updated)
    out_stage[pl.ds(6, DEV, stride=8), :] = dot(by_owner_ref[...], total.astype(BF))
    out_stage[pl.ds(7, DEV, stride=8), :] = jnp.zeros((DEV, BLK), F32)
    out_ref[...] = out_stage[...].astype(BF)


def unpack_kernel(recv_ref, grad_hbm, mask_hbm, stage, wide, grad, sem):
    stage[...] = recv_ref[...].astype(F32)
    for r in range(ROWS):
        grad[pl.ds(r, COLS, stride=ROWS), :] = stage[pl.ds(r * COLS * 8 + 6, COLS, stride=8), :]
    copies = [pltpu.make_async_copy(grad, grad_hbm, sem.at[3])]
    copies[0].start()
    for q in range(3):
        for r in range(ROWS):
            for p in range(2):
                wide[q, pl.ds(p * BLK + r, COLS, stride=ROWS), :] = stage[
                    pl.ds(r * COLS * 8 + 3 * p + q, COLS, stride=8), :
                ]
        here = pl.ds(q * BLK, BLK)
        copies.append(pltpu.make_async_copy(wide.at[q], mask_hbm.at[:, here], sem.at[q]))
        copies[q + 1].start()
    for copy in copies:
        copy.wait()


SMEM = pl.BlockSpec(memory_space=pltpu.SMEM)
VMEM = pl.BlockSpec(memory_space=pltpu.VMEM)
HBM = pl.BlockSpec(memory_space=pltpu.HBM)


def call(kernel, out_shape, in_specs, scratch, limit=8, out_space=None):
    return pl.pallas_call(
        kernel,
        out_shape=out_shape,
        in_specs=in_specs,
        out_specs=out_space or jax.tree.map(lambda _: VMEM, out_shape),
        scratch_shapes=scratch,
        compiler_params=pltpu.CompilerParams(vmem_limit_bytes=limit << 20),
    )


def in_hbm(x):
    return pltpu.with_memory_space_constraint(x, pltpu.HBM)


def exchange(x, axes=AXES):
    return lax.all_to_all(x, axes, 0, 0, tiled=True)


def per_device(cells, target, row_taps, col_taps, socs, cell_of_block, owner_map):
    struct = jax.ShapeDtypeStruct
    place = jnp.stack([lax.axis_index("row"), lax.axis_index("col")]).astype(jnp.int32)
    owner = owner_map.reshape(1, DEV)

    def spread(taps, reverse):
        flat = taps.reshape(2 * CHAN, 2 * HALF + 1).astype(F32)
        gap = jnp.zeros((2 * CHAN, 2 * BLK - 2 * HALF - 1), F32)
        if reverse:
            return jnp.concatenate([flat[:, :1], gap, flat[:, :0:-1]], 1)
        return jnp.concatenate([flat, gap], 1)

    down = [(i, i + 1) for i in range(ROWS - 1)]
    up = [(i + 1, i) for i in range(ROWS - 1)]
    above = lax.ppermute(target[TILE_R - HALF :], "row", down)
    below = lax.ppermute(target[:HALF], "row", up)
    wide_target = jnp.concatenate(
        [
            above,
            target,
            below,
            jnp.zeros((FIELD_R - TILE_R - 2 * HALF, TILE_C), F32),
        ],
        0,
    )

    select = struct((DEV, DEV), BF)
    first, by_cell, by_owner = call(
        pack_kernel,
        (struct((DEV * 8, BLK), BF), select, select),
        [HBM, HBM, HBM],
        [
            pltpu.SMEM((2, 3), jnp.int32),
            pltpu.VMEM((1, DEV), jnp.int32),
            pltpu.VMEM((BLK, BLK), F32),
            pltpu.VMEM((COLS * 8, BLK), F32),
            pltpu.VMEM((COLS * 8, BLK), BF),
            pltpu.SemaphoreType.DMA,
            pltpu.SemaphoreType.DMA,
            pltpu.SemaphoreType.DMA,
            pltpu.SemaphoreType.DMA((ROWS,)),
        ],
        out_space=(HBM, VMEM, VMEM),
    )(in_hbm(cell_of_block), in_hbm(cells.reshape(BLK, BLK)), in_hbm(owner))
    first = exchange(first.reshape(DEV, 8, BLK))
    first = first.reshape(DEV * 8, BLK)

    picked, held, slots = call(
        pick_kernel,
        (struct((COLS * PER_COL, BLK), BF), struct((BLK, BLK), F32), struct((DEV, BLK), F32)),
        [SMEM, VMEM, VMEM],
        [
            pltpu.VMEM((DEV * 8, BLK), F32),
            pltpu.VMEM((COLS, BLK), F32),
            pltpu.VMEM((COLS * PER_COL, BLK), F32),
            pltpu.VMEM((COLS * PER_COL, BLK), BF),
            pltpu.SemaphoreType.DMA((ROWS,)),
        ],
        out_space=(HBM, VMEM, VMEM),
    )(place, first, by_cell)
    received = exchange(picked.reshape(COLS, PER_COL, BLK), "col")
    received = received.reshape(COLS * PER_COL, BLK)

    pieces = call(
        litho_kernel,
        struct((DEV * SLOTS, BLK), BF),
        [SMEM] * 2 + [VMEM] * 6,
        [
            pltpu.VMEM((COLS * PER_COL, BLK), F32),
            pltpu.VMEM((4, 384, BLK), F32),
            pltpu.VMEM((COL_R, 512), BF),
            pltpu.VMEM((2, COL_ROWS, TILE_C), BF),
            pltpu.VMEM((2, COL_ROWS, TILE_C), BF),
            pltpu.VMEM((CHAN, FIELD_R, TILE_C), F32),
            pltpu.VMEM((FIELD_R, TILE_C), F32),
            pltpu.VMEM((TILE_R, 512), F32),
            pltpu.VMEM((TILE_R, 12 * BLK), BF),
            pltpu.VMEM((TILE_R, 12 * BLK), BF),
        ],
        32,
    )(
        place, in_hbm(socs), received, wide_target,
        spread(row_taps, False), spread(row_taps[:, :, ::-1], False),
        spread(col_taps, False), spread(col_taps, True),
    )
    pieces = exchange(pieces.reshape(DEV, SLOTS, BLK)).reshape(DEV * SLOTS, BLK)

    results = call(
        update_kernel,
        struct((DEV * 8, BLK), BF),
        [VMEM] * 4,
        [pltpu.VMEM((DEV * SLOTS, BLK), F32), pltpu.VMEM((DEV * 8, BLK), F32)],
    )(pieces, slots, by_owner, held)
    results = exchange(results.reshape(DEV, 8, BLK)).reshape(DEV * 8, BLK)

    gradient, new_mask = call(
        unpack_kernel,
        (struct((BLK, BLK), F32), struct((TILE_R, TILE_C), F32)),
        [VMEM],
        [
            pltpu.VMEM((DEV * 8, BLK), F32),
            pltpu.VMEM((3, TILE_R, BLK), F32),
            pltpu.VMEM((BLK, BLK), F32),
            pltpu.SemaphoreType.DMA((4,)),
        ],
        out_space=(HBM, HBM),
    )(results)
    return gradient.reshape(1, BLK, BLK), new_mask


def solution(mesh):
    in_specs = (P(AXES, None, None), P("row", "col"), P(), P(), P(), P("row", "col"), P())
    out_specs = (P(AXES, None, None), P("row", "col"))
    return jax.shard_map(
        per_device, mesh=mesh, in_specs=in_specs, out_specs=out_specs, check_vma=False
    )
```
